32 devices in a mesh: fsdp: 32 (over z, y, x, core).
Axes of the slice: x: 2, y: 2, z: 4, core: 2. Of those that a mesh axis runs over, the one named last changes fastest.
Arguments:
- tokens: bfloat16 [32768, 640], P('fsdp'), may hold values from -6 to 6
- cotangent: bfloat16 [32768, 640], P('fsdp'), may hold values from -6 to 6
- seq_lens: int32 [128], P('fsdp'), may hold values from 0 to 1024, as said below
- seq_starts: int32 [128], P('fsdp'), may hold values from 0 to 1024, as said below
- input_gain: bfloat16 [640], P('fsdp'), may hold values from 0.099609375 to 1.8984375
- w_query: bfloat16 [640, 1024], P('fsdp'), may hold values from -0.25 to 0.25
- w_key: bfloat16 [640, 256], P('fsdp'), may hold values from -0.25 to 0.25
- w_value: bfloat16 [640, 256], P('fsdp'), may hold values from -0.25 to 0.25
- query_gain: bfloat16 [256], P('fsdp'), may hold values from 0.099609375 to 1.8984375
- key_gain: bfloat16 [256], P('fsdp'), may hold values from 0.099609375 to 1.8984375
- w_output: bfloat16 [1024, 640], P('fsdp'), may hold values from -0.1875 to 0.1875
- attn_post_gain: bfloat16 [640], P('fsdp'), may hold values from 0.099609375 to 1.8984375
- ffn_pre_gain: bfloat16 [640], P('fsdp'), may hold values from 0.099609375 to 1.8984375
- w_gate: bfloat16 [640, 2048], P('fsdp'), may hold values from -0.25 to 0.25
- w_up: bfloat16 [640, 2048], P('fsdp'), may hold values from -0.25 to 0.25
- w_down: bfloat16 [2048, 640], P('fsdp'), may hold values from -0.125 to 0.125
- ffn_post_gain: bfloat16 [640], P('fsdp'), may hold values from 0.099609375 to 1.8984375
Outputs:
- result: bfloat16 [32768, 640], P('fsdp')
- grad_tokens: float32 [32768, 640], P('fsdp')
- grad_input_gain: float32 [640], P('fsdp')
- grad_w_query: float32 [640, 1024], P('fsdp')
- grad_w_key: float32 [640, 256], P('fsdp')
- grad_w_value: float32 [640, 256], P('fsdp')
- grad_query_gain: float32 [256], P('fsdp')
- grad_key_gain: float32 [256], P('fsdp')
- grad_w_output: float32 [1024, 640], P('fsdp')
- grad_attn_post_gain: float32 [640], P('fsdp')
- grad_ffn_pre_gain: float32 [640], P('fsdp')
- grad_w_gate: float32 [640, 2048], P('fsdp')
- grad_w_up: float32 [640, 2048], P('fsdp')
- grad_w_down: float32 [2048, 640], P('fsdp')
- grad_ffn_post_gain: float32 [640], P('fsdp')
The draws below stay inside these ranges and needn't reach their ends.
Inputs may be any that keep to these rules, and one draw needn't show every extreme that they name: `seq_lens`: on each device its 4 sequence slots lie end to end from token slot 0 in the order given, so seq_starts is the sum of the lengths before it on that device; a length may be 0; every device has 256 or more slots inside sequences; some device holds one sequence of exactly 1024 tokens, filling it. `seq_starts`: the start of each sequence slot, as described for seq_lens.
All inputs are finite; a program needn't handle non-finite values.
Results may differ from the reference program's by a relative error of at most 0.017.
Values may be sent and summed in bfloat16 or wider, within the bound.
No kernel may reach another device: no remote copies, remote signals or barrier semaphores. Data moves between devices by JAX's collectives and lax.ppermute only.
A program may use at most 192 MiB of HBM per device.

```python
import jax
import jax.numpy as jnp
from jax import lax

D = 640
HQ = 4
HD = 256
FF = 2048
TOK_DEV = 1024
SEQ_DEV = 4
TOKENS = 32768
SEQS = 128


def packing(key):
    devices = SEQS // SEQ_DEV
    key_count, key_full, key_split = jax.random.split(jax.random.fold_in(key, 11), 3)
    counts = jax.random.randint(key_count, (devices,), TOK_DEV // 4, TOK_DEV + 1)
    chosen = jax.random.randint(key_full, (), 0, devices)
    filled = jnp.arange(devices) == chosen
    counts = jnp.where(filled, TOK_DEV, counts)
    splits = jax.random.randint(key_split, (devices, SEQ_DEV - 1), 0, TOK_DEV + 1) * counts[:, None] // TOK_DEV
    splits = jnp.where(filled[:, None], TOK_DEV, splits)
    splits = jnp.sort(splits, axis=1)
    bounds = jnp.concatenate([jnp.zeros((devices, 1), jnp.int32), splits.astype(jnp.int32), counts[:, None].astype(jnp.int32)], axis=1)
    lengths = bounds[:, 1:] - bounds[:, :-1]
    return (lengths.reshape(-1).astype(jnp.int32), bounds[:, :-1].reshape(-1).astype(jnp.int32))


def draw_seq_lens(key, part):
    return packing(key)[0]


def draw_seq_starts(key, part):
    return packing(key)[1]


def with_spikes(values, rng, source, target, shards_of, factor):
    owner, partner = [(jnp.arange(values.shape[dim]) // (values.shape[dim] // shards_of)).reshape([-1 if axis == dim else 1 for axis in range(values.ndim)]) for dim in (source, target)]
    chosen = jax.random.permutation(rng, shards_of)[partner]
    strong = (owner == chosen) | (owner == (partner + shards_of // 2) % shards_of)
    return jnp.where(strong, factor * values, values)


def shard_levels(key, extent, pieces, smallest, high):
    gain = 1.0
    for dim, blocks in pieces:
        steps = jax.random.uniform(jax.random.fold_in(jax.random.fold_in(key, 6), dim), (blocks,), jnp.float32, smallest / len(pieces), high / len(pieces))
        gain = gain * jnp.repeat(jnp.exp(steps), extent[dim] // blocks).reshape((-1,) + (1,) * (len(extent) - 1 - dim))
    return gain


def noise(own_key, extent, width, most, cuts=(), kind=jnp.bfloat16):
    drawn = jax.random.normal(own_key, extent, jnp.float32) * width
    if len(cuts) > 0:
        drawn = shard_levels(own_key, extent, cuts, -0.22, 0.18) * drawn
    return jnp.clip(drawn, min=-most, max=most).astype(kind)


def bell_draw_with(key, shape, deviation, limit, shards, heavy, held_as=jnp.bfloat16):
    drawn = deviation * jax.random.normal(key, shape, jnp.float32)
    if shards:
        drawn = drawn * shard_levels(key, shape, shards, -0.22, 0.18)
    return jnp.clip(with_spikes(drawn, jax.random.fold_in(key, 3), *heavy), -limit, limit).astype(held_as)


def setup_inputs(seed: int = 0) -> dict:
    key_list = jax.random.split(jax.random.key(seed), 18)
    return {
        "tokens": noise(key_list[0], (TOKENS, D), 1.0, 6.0, ((0, 32),)),
        "cotangent": bell_draw_with(key_list[1], (TOKENS, D), 1.0, 6.0, ((0, 32),), (0, 1, 32, 2.75)),
        "seq_lens": draw_seq_lens(jax.random.fold_in(key_list[17], 71), 0),
        "seq_starts": draw_seq_starts(jax.random.fold_in(key_list[17], 71), 0),
        "input_gain": jnp.clip(1.0 + 0.18 * jax.random.normal(key_list[4], (D,), jnp.float32), 0.099609375, 1.8984375).astype(jnp.bfloat16),
        "w_query": noise(key_list[5], (D, HQ * HD), D ** -0.5, 0.25, ((0, 32),)),
        "w_key": noise(key_list[6], (D, HD), D ** -0.5, 0.25, ((0, 32),)),
        "w_value": noise(key_list[7], (D, HD), D ** -0.5, 0.25, ((0, 32),)),
        "query_gain": jnp.clip(1.0 + 0.18 * jax.random.normal(key_list[8], (HD,), jnp.float32), 0.099609375, 1.8984375).astype(jnp.bfloat16),
        "key_gain": jnp.clip(1.0 + 0.18 * jax.random.normal(key_list[9], (HD,), jnp.float32), 0.099609375, 1.8984375).astype(jnp.bfloat16),
        "w_output": noise(key_list[10], (HQ * HD, D), (HQ * HD) ** -0.5, 0.1875, ((0, 32),)),
        "attn_post_gain": jnp.clip(1.0 + 0.18 * jax.random.normal(key_list[11], (D,), jnp.float32), 0.099609375, 1.8984375).astype(jnp.bfloat16),
        "ffn_pre_gain": jnp.clip(1.0 + 0.18 * jax.random.normal(key_list[12], (D,), jnp.float32), 0.099609375, 1.8984375).astype(jnp.bfloat16),
        "w_gate": noise(key_list[13], (D, FF), D ** -0.5, 0.25, ((0, 32),)),
        "w_up": noise(key_list[14], (D, FF), D ** -0.5, 0.25, ((0, 32),)),
        "w_down": noise(key_list[15], (FF, D), FF ** -0.5, 0.125, ((0, 32),)),
        "ffn_post_gain": jnp.clip(1.0 + 0.18 * jax.random.normal(key_list[16], (D,), jnp.float32), 0.099609375, 1.8984375).astype(jnp.bfloat16),
    }


epsilon = 1e-06
rope_base = 1000000.0

@jax.custom_vjp
def low(v):
    return lax.optimization_barrier(v.astype(jnp.bfloat16)).astype(jnp.float32)

@jax.custom_vjp
def low_back(v):
    return v

def low_keep(v):
    return (low(v), None)

def low_pass(kept, grad):
    return (grad,)

def back_keep(v):
    return (v, None)

def back_low(kept, grad):
    return (low(grad),)
low.defvjp(low_keep, low_pass)
low_back.defvjp(back_keep, back_low)

def multiply(left_side, right_side):
    return jnp.dot(left_side, right_side, precision=lax.Precision.HIGHEST, preferred_element_type=jnp.float32)

def rms_scale(vector_rows, gain_row):
    return vector_rows * lax.rsqrt(lax.optimization_barrier(jnp.mean(vector_rows * vector_rows, axis=-1, keepdims=True)) + epsilon) * gain_row

def rotate(vector_rows, positions):
    half_width = vector_rows.shape[-1] // 2
    frequency = rope_base ** (-2.0 * jnp.arange(half_width, dtype=jnp.float32) / vector_rows.shape[-1])
    angles = positions[:, None] * frequency[None, :]
    if vector_rows.ndim == 3:
        angles = angles[:, None, :]
    cosine = jnp.cos(angles)
    sine_part = jnp.sin(angles)
    first_half = vector_rows[..., :half_width]
    second_half = vector_rows[..., half_width:]
    return jnp.concatenate([first_half * cosine - second_half * sine_part, second_half * cosine + first_half * sine_part], axis=-1)

def prep_query(raw_rows, gain_row, positions):
    shaped = raw_rows.reshape(raw_rows.shape[0], -1, gain_row.shape[0])
    return rotate(rms_scale(shaped, gain_row), positions) * 0.0625

def prep_key(raw_rows, gain_row, positions):
    return rotate(rms_scale(raw_rows, gain_row), positions)

def layout(lengths, starts, slot_count):
    slot_index = jnp.arange(slot_count, dtype=jnp.int32)
    inside = (slot_index[None, :] >= starts[:, None]) & (slot_index[None, :] < starts[:, None] + lengths[:, None])
    member = inside.astype(jnp.float32)
    live_mask = lax.optimization_barrier(jnp.sum(member, axis=0))
    offset = lax.optimization_barrier(jnp.sum(member * starts[:, None].astype(jnp.float32), axis=0))
    positions = slot_index.astype(jnp.float32) - offset
    same_seq = jnp.dot(member.T, member, preferred_element_type=jnp.float32) > 0.5
    allowed = same_seq & (slot_index[None, :] <= slot_index[:, None]) | (slot_index[None, :] == slot_index[:, None])
    return (live_mask, positions, allowed)

def attend_block(operands):
    queries, key_rows, value_rows, allowed = operands
    scores = low_back(jnp.einsum('thd,ud->htu', queries, key_rows, precision=lax.Precision.HIGHEST, preferred_element_type=jnp.float32))
    masked = jnp.where(allowed[None], scores, -1e+30)
    row_peak = lax.optimization_barrier(jnp.max(masked, axis=-1, keepdims=True))
    exponent = jnp.exp(masked - row_peak)
    probability = exponent / lax.optimization_barrier(jnp.sum(exponent, axis=-1, keepdims=True))
    return jnp.einsum('htu,ud->thd', low(probability), value_rows, precision=lax.Precision.HIGHEST, preferred_element_type=jnp.float32)

def reference(tokens, cotangent, seq_lens, seq_starts, input_gain, w_query, w_key, w_value, query_gain, key_gain, w_output, attn_post_gain, ffn_pre_gain, w_gate, w_up, w_down, ffn_post_gain):
    slot_count = TOK_DEV
    blocks = tokens.shape[0] // slot_count

    def block_layout(lengths, starts):
        return layout(lengths, starts, slot_count)
    live_mask, positions, allowed = jax.vmap(block_layout)(seq_lens.reshape(blocks, SEQ_DEV), seq_starts.reshape(blocks, SEQ_DEV))
    live_mask = live_mask.reshape(-1)
    positions = positions.reshape(-1)
    params = (input_gain.astype(jnp.float32), w_query.astype(jnp.float32), w_key.astype(jnp.float32), w_value.astype(jnp.float32), query_gain.astype(jnp.float32), key_gain.astype(jnp.float32), w_output.astype(jnp.float32), attn_post_gain.astype(jnp.float32), ffn_pre_gain.astype(jnp.float32), w_gate.astype(jnp.float32), w_up.astype(jnp.float32), w_down.astype(jnp.float32), ffn_post_gain.astype(jnp.float32))

    def forward(inputs, weights):
        gain_in, query_w, key_w, value_w, gain_q, gain_k, output_w, gain_post, gain_pre, gate_w, up_w, down_w, gain_ffn = weights
        normed = low(rms_scale(inputs, gain_in))
        query_raw = low_back(multiply(normed, query_w))
        key_raw = low_back(multiply(normed, key_w))
        value_low = low(low_back(multiply(normed, value_w)))
        query_low = low(prep_query(query_raw, gain_q, positions))
        key_low = low(prep_key(key_raw, gain_k, positions))
        mixture = lax.map(jax.checkpoint(attend_block), (query_low.reshape(blocks, slot_count, HQ, HD), key_low.reshape(blocks, slot_count, HD), value_low.reshape(blocks, slot_count, HD), allowed))
        mixed_low = low(low_back(mixture.reshape(-1, HQ * HD)))
        attn_out = low_back(multiply(mixed_low, output_w))
        middle = inputs + rms_scale(attn_out, gain_post)
        normed_ffn = low(rms_scale(middle, gain_pre))
        gating = low_back(multiply(normed_ffn, gate_w))
        upward = low_back(multiply(normed_ffn, up_w))
        active = low(jax.nn.gelu(gating, approximate=True) * upward)
        down_out = low_back(multiply(active, down_w))
        output_rows = middle + rms_scale(down_out, gain_ffn)
        return output_rows * live_mask[:, None]
    output_rows, pullback = jax.vjp(forward, tokens.astype(jnp.float32), params)
    grad_inputs, gradients = pullback(cotangent.astype(jnp.float32))
    return (output_rows.astype(jnp.bfloat16), grad_inputs, gradients[0], gradients[1], gradients[2], gradients[3], gradients[4], gradients[5], gradients[6], gradients[7], gradients[8], gradients[9], gradients[10], gradients[11], gradients[12])
```

```python
import jax
import jax.numpy as jnp
from jax import lax
from jax.sharding import PartitionSpec as P

AX = "fsdp"
epsilon = 1e-06
rope_base = 1000000.0
BF = jnp.bfloat16
F32 = jnp.float32
LANES = 128


def product(left_side, right_side):
    return jnp.dot(left_side, right_side, preferred_element_type=jnp.float32)


def times_transposed(left_side, right_side):
    return lax.dot_general(
        left_side, right_side, (((1,), (1,)), ((), ())), preferred_element_type=jnp.float32
    )


def outer_sum(left_side, right_side):
    return lax.dot_general(
        left_side, right_side, (((0,), (0,)), ((), ())), preferred_element_type=jnp.float32
    )


def rms_scale(vector_rows, gain_row):
    return (
        vector_rows
        * lax.rsqrt(jnp.mean(vector_rows * vector_rows, axis=-1, keepdims=True) + epsilon)
        * gain_row
    )


def rotate(vector_rows, positions):
    half_width = vector_rows.shape[-1] // 2
    frequency = rope_base ** (
        -2.0 * jnp.arange(half_width, dtype=jnp.float32) / vector_rows.shape[-1]
    )
    angles = positions[:, None] * frequency[None, :]
    if vector_rows.ndim == 3:
        angles = angles[:, None, :]
    cosine = jnp.cos(angles)
    sine_part = jnp.sin(angles)
    first_half = vector_rows[..., :half_width]
    second_half = vector_rows[..., half_width:]
    return jnp.concatenate(
        [
            first_half * cosine - second_half * sine_part,
            second_half * cosine + first_half * sine_part,
        ],
        axis=-1,
    )


def prep_query(raw_rows, gain_row, positions):
    shaped = raw_rows.reshape(raw_rows.shape[0], -1, gain_row.shape[0])
    return rotate(rms_scale(shaped, gain_row), positions) * 0.0625


def prep_key(raw_rows, gain_row, positions):
    return rotate(rms_scale(raw_rows, gain_row), positions)


def glu_mix(gating, upward):
    return jax.nn.gelu(gating, approximate=True) * upward


def layout(lengths, starts, slot_count):
    slot_index = jnp.arange(slot_count, dtype=jnp.int32)
    inside = (slot_index[None, :] >= starts[:, None]) & (
        slot_index[None, :] < starts[:, None] + lengths[:, None]
    )
    member = inside.astype(jnp.float32)
    live_mask = jnp.sum(member, axis=0)
    offset = jnp.sum(member * starts[:, None].astype(jnp.float32), axis=0)
    positions = slot_index.astype(jnp.float32) - offset
    same_seq = jnp.dot(member.T, member, preferred_element_type=jnp.float32) > 0.5
    allowed = same_seq & (slot_index[None, :] <= slot_index[:, None]) | (
        slot_index[None, :] == slot_index[:, None]
    )
    return (live_mask, positions, allowed)


def attend(queries, key_rows, value_rows, allowed):
    scores = jnp.einsum("thd,ud->htu", queries, key_rows, preferred_element_type=jnp.float32)
    masked = jnp.where(allowed[None], scores, -1e30)
    row_peak = jnp.max(masked, axis=-1, keepdims=True)
    exponent = jnp.exp(masked - row_peak)
    row_total = jnp.sum(exponent, axis=-1, keepdims=True)
    probability = (exponent / row_total).astype(jnp.bfloat16)
    mixture = jnp.einsum("htu,ud->thd", probability, value_rows, preferred_element_type=jnp.float32)
    return (mixture, row_peak + jnp.log(row_total))


def attend_back(queries, key_rows, value_rows, allowed, log_total, grad_mixture):
    scores = jnp.einsum("thd,ud->htu", queries, key_rows, preferred_element_type=jnp.float32)
    masked = jnp.where(allowed[None], scores, -1e30)
    probability = jnp.exp(masked - log_total)
    weights_low = probability.astype(jnp.bfloat16)
    grad_probs = jnp.einsum(
        "thd,ud->htu", grad_mixture, value_rows, preferred_element_type=jnp.float32
    )
    grad_values = jnp.einsum(
        "htu,thd->ud", weights_low, grad_mixture, preferred_element_type=jnp.float32
    )
    row_inner = jnp.sum(probability * grad_probs, axis=-1, keepdims=True)
    grad_scores = (probability * (grad_probs - row_inner)).astype(jnp.bfloat16)
    grad_queries = jnp.einsum(
        "htu,ud->thd", grad_scores, key_rows, preferred_element_type=jnp.float32
    )
    grad_keys = jnp.einsum("htu,thd->ud", grad_scores, queries, preferred_element_type=jnp.float32)
    return (grad_queries, grad_keys, grad_values)


class Mover:
    def __init__(self, device_count):
        self.n = device_count
        self.chips = device_count // 2
        self.digits = 0
        while 4 ** (self.digits + 1) <= self.chips:
            self.digits += 1
        self.me = lax.axis_index(AX)
        self.core = self.me % 2
        self.chip = self.me // 2

    def swap(self, value, mask=1):
        return lax.ppermute(value, AX, [(i, i ^ mask) for i in range(self.n)])

    def in_core_order(self, mine, other):
        first = self.core == 0
        return jnp.where(first, mine, other), jnp.where(first, other, mine)

    def gather(self, narrow, tall, gains):
        rows = narrow[0].shape[0]
        halves = [jnp.split(w, 2, axis=1) for w in narrow]
        low = jnp.concatenate([h[0] for h in halves], axis=1)
        high = jnp.concatenate([h[1] for h in halves], axis=1)
        first = self.core == 0
        mine = jnp.where(first, low, high)
        other = self.swap(jnp.where(first, high, low))
        both = jnp.concatenate(self.in_core_order(mine, other), axis=0)
        tiles = both.reshape(2 * rows, -1, LANES).transpose(1, 0, 2).reshape(-1, LANES)
        parts = [tiles]
        for w in tall:
            parts.append(w.reshape(w.shape[0], -1, LANES).transpose(1, 0, 2).reshape(-1, LANES))
        if gains:
            flat = jnp.concatenate(gains)
            parts.append(jnp.pad(flat, (0, 8 * LANES - flat.shape[0])).reshape(8, LANES))
        whole = lax.all_gather(jnp.concatenate(parts, axis=0), AX, axis=0)
        whole = whole.reshape(self.chips, 2, -1, LANES)
        at = 0
        out_narrow, out_tall, out_gains = [], [], []
        for w in narrow:
            t = w.shape[1] // (2 * LANES)
            piece = whole[:, :, at : at + t * 2 * rows].reshape(self.chips, 2, t, 2 * rows, LANES)
            out_narrow.append(piece.transpose(0, 3, 1, 2, 4).reshape(self.n * rows, w.shape[1]))
            at += t * 2 * rows
        for w in tall:
            t = w.shape[1] // LANES
            piece = whole[:, :, at : at + t * w.shape[0]].reshape(self.n, t, w.shape[0], LANES)
            out_tall.append(piece.transpose(0, 2, 1, 3).reshape(self.n * w.shape[0], w.shape[1]))
            at += t * w.shape[0]
        if gains:
            piece = whole[:, :, at:].reshape(self.n, 8 * LANES)
            start = 0
            for g in gains:
                out_gains.append(piece[:, start : start + g.shape[0]].reshape(-1).astype(F32))
                start += g.shape[0]
        return out_narrow, out_tall, out_gains

    def reduce(self, narrow, tall, gains):
        parts = []
        for g in narrow:
            rows = g.shape[0] // self.chips
            t = g.shape[1] // (2 * LANES)
            piece = g.astype(BF).reshape(self.chips, rows, 2, t, LANES).transpose(2, 0, 3, 1, 4)
            parts.append(piece.reshape(2, self.chips, t * rows, LANES))
        for g in tall:
            rows = g.shape[0] // self.n
            t = g.shape[1] // LANES
            piece = g.astype(BF).reshape(self.chips, 2, rows, t, LANES).transpose(1, 0, 3, 2, 4)
            parts.append(piece.reshape(2, self.chips, t * rows, LANES))
        if gains:
            flat = jnp.concatenate([g.reshape(self.n, -1) for g in gains], axis=1).astype(BF)
            flat = jnp.pad(flat, ((0, 0), (0, 8 * LANES - flat.shape[1])))
            parts.append(flat.reshape(self.chips, 2, 8, LANES).transpose(1, 0, 2, 3))
        packed = jnp.concatenate(parts, axis=2)
        keep = lax.dynamic_index_in_dim(packed, self.core, 0, keepdims=False)
        send = lax.dynamic_index_in_dim(packed, 1 - self.core, 0, keepdims=False)
        total = keep.astype(F32) + self.swap(send).astype(F32)
        for digit in range(self.digits):
            low = total.astype(BF).reshape(total.shape[0] // 4, 4, -1, LANES)
            here = (self.chip >> (2 * digit)) % 4
            moved = [
                self.swap(
                    lax.dynamic_index_in_dim(low, here ^ j, 1, keepdims=False),
                    j << (2 * digit + 1),
                )
                for j in (1, 2, 3)
            ]
            total = lax.dynamic_index_in_dim(
                total.reshape(low.shape), here, 1, keepdims=False
            )
            for m in moved:
                total = total + m.astype(F32)
        total = total[0]
        at = 0
        outs = []
        count = sum(g.shape[0] // self.chips * (g.shape[1] // (2 * LANES)) for g in narrow)
        if narrow:
            rows = narrow[0].shape[0] // self.n
            tiles = total[:count].reshape(-1, 2, rows, LANES)
            mine = lax.dynamic_index_in_dim(tiles, self.core, 1, keepdims=False)
            other = self.swap(lax.dynamic_index_in_dim(tiles, 1 - self.core, 1, keepdims=False))
            halves = self.in_core_order(mine, other)
            for g in narrow:
                t = g.shape[1] // (2 * LANES)
                both = jnp.stack([h[at : at + t] for h in halves])
                outs.append(both.transpose(2, 0, 1, 3).reshape(rows, g.shape[1]))
                at += t
        at = count
        for g in tall:
            rows = g.shape[0] // self.n
            t = g.shape[1] // LANES
            outs.append(
                total[at : at + t * rows].reshape(t, rows, LANES).transpose(1, 0, 2).reshape(rows, -1)
            )
            at += t * rows
        if gains:
            flat = total[at:].reshape(-1)
            start = 0
            for g in gains:
                own = g.shape[0] // self.n
                outs.append(flat[start : start + own])
                start += own
        return outs


def on_device(
    device_count,
    tokens,
    cotangent,
    seq_lens,
    seq_starts,
    input_gain,
    w_query,
    w_key,
    w_value,
    query_gain,
    key_gain,
    w_output,
    attn_post_gain,
    ffn_pre_gain,
    w_gate,
    w_up,
    w_down,
    ffn_post_gain,
):
    mover = Mover(device_count)
    slot_count = tokens.shape[0]
    live_mask, positions, allowed = layout(seq_lens, seq_starts, slot_count)
    (query_w, key_w, value_w), _, gains = mover.gather(
        [w_query, w_key, w_value],
        [],
        [input_gain, query_gain, key_gain, attn_post_gain, ffn_pre_gain, ffn_post_gain],
    )
    gain_in, gain_q, gain_k, gain_post, gain_pre, gain_ffn = gains
    (gate_w, up_w), (output_w, down_w), _ = mover.gather([w_gate, w_up], [w_output, w_down], [])
    head_count = query_w.shape[1] // key_w.shape[1]

    def query_piece(raw_rows, gain_row):
        return prep_query(raw_rows, gain_row, positions)

    def key_piece(raw_rows, gain_row):
        return prep_key(raw_rows, gain_row, positions)

    inputs = tokens.astype(jnp.float32)
    normed = rms_scale(inputs, gain_in).astype(jnp.bfloat16)
    query_raw = product(normed, query_w)
    key_raw = product(normed, key_w)
    value_low = product(normed, value_w).astype(jnp.bfloat16)
    query_low = query_piece(query_raw, gain_q).astype(jnp.bfloat16)
    key_low = key_piece(key_raw, gain_k).astype(jnp.bfloat16)
    mixture, log_total = attend(query_low, key_low, value_low, allowed)
    mixed_low = mixture.reshape(slot_count, -1).astype(jnp.bfloat16)
    attn_out = product(mixed_low, output_w)
    middle = inputs + rms_scale(attn_out, gain_post)
    normed_ffn = rms_scale(middle, gain_pre).astype(jnp.bfloat16)
    gating = product(normed_ffn, gate_w)
    upward = product(normed_ffn, up_w)
    active = glu_mix(gating, upward).astype(jnp.bfloat16)
    down_out = product(active, down_w)
    output_rows = middle + rms_scale(down_out, gain_ffn)
    result = (live_mask[:, None] * output_rows).astype(jnp.bfloat16)
    grad_output = cotangent.astype(jnp.float32) * live_mask[:, None]
    _, post_ffn_back = jax.vjp(rms_scale, down_out, gain_ffn)
    grad_down_out, grad_gain_ffn = post_ffn_back(grad_output)
    grad_down_low = grad_down_out.astype(jnp.bfloat16)
    grad_active = times_transposed(grad_down_low, down_w)
    part_down = outer_sum(active, grad_down_low)
    _, glu_back = jax.vjp(glu_mix, gating, upward)
    grad_gating, grad_upward = glu_back(grad_active)
    grad_gate_low = grad_gating.astype(jnp.bfloat16)
    grad_up_low = grad_upward.astype(jnp.bfloat16)
    part_gate = outer_sum(normed_ffn, grad_gate_low)
    part_up = outer_sum(normed_ffn, grad_up_low)
    grad_normed_ffn = times_transposed(grad_gate_low, gate_w) + times_transposed(grad_up_low, up_w)
    _, pre_ffn_back = jax.vjp(rms_scale, middle, gain_pre)
    grad_middle_part, grad_gain_pre = pre_ffn_back(grad_normed_ffn)
    grad_middle = grad_output + grad_middle_part
    _, post_attn_back = jax.vjp(rms_scale, attn_out, gain_post)
    grad_attn_out, grad_gain_post = post_attn_back(grad_middle)
    grad_attn_low = grad_attn_out.astype(jnp.bfloat16)
    part_output = outer_sum(mixed_low, grad_attn_low)
    own_gate, own_up, own_output, own_down = mover.reduce(
        [part_gate, part_up], [part_output, part_down], []
    )
    grad_mixture = (
        times_transposed(grad_attn_low, output_w)
        .astype(jnp.bfloat16)
        .reshape(slot_count, head_count, -1)
    )
    grad_queries, grad_keys, grad_values = attend_back(
        query_low, key_low, value_low, allowed, log_total, grad_mixture
    )
    grad_value_low = grad_values.astype(jnp.bfloat16)
    _, query_back = jax.vjp(query_piece, query_raw, gain_q)
    grad_query_raw, grad_gain_q = query_back(grad_queries)
    _, key_back = jax.vjp(key_piece, key_raw, gain_k)
    grad_key_raw, grad_gain_k = key_back(grad_keys)
    grad_query_low = grad_query_raw.astype(jnp.bfloat16)
    grad_key_low = grad_key_raw.astype(jnp.bfloat16)
    part_query = outer_sum(normed, grad_query_low)
    part_key = outer_sum(normed, grad_key_low)
    part_value = outer_sum(normed, grad_value_low)
    grad_normed = (
        times_transposed(grad_query_low, query_w)
        + times_transposed(grad_key_low, key_w)
        + times_transposed(grad_value_low, value_w)
    )
    _, input_back = jax.vjp(rms_scale, inputs, gain_in)
    grad_inputs_part, grad_gain_in = input_back(grad_normed)
    grad_tokens = grad_middle + grad_inputs_part
    (own_query, own_key, own_value, own_gin, own_gq, own_gk, own_gpost, own_gpre, own_gffn) = (
        mover.reduce(
            [part_query, part_key, part_value],
            [],
            [grad_gain_in, grad_gain_q, grad_gain_k, grad_gain_post, grad_gain_pre, grad_gain_ffn],
        )
    )
    return (
        result,
        grad_tokens,
        own_gin,
        own_query,
        own_key,
        own_value,
        own_gq,
        own_gk,
        own_output,
        own_gpost,
        own_gpre,
        own_gate,
        own_up,
        own_down,
        own_gffn,
    )


def solution(mesh):
    rows, flat = P(AX, None), P(AX)
    device_count = mesh.shape[AX]

    def block(*arrays):
        return on_device(device_count, *arrays)

    return jax.shard_map(
        block,
        mesh=mesh,
        in_specs=(
            rows, rows, flat, flat, flat, rows, rows, rows, flat, flat, rows, flat, flat, rows, rows, rows, flat,
        ),
        out_specs=(
            rows, rows, flat, rows, rows, rows, flat, flat, rows, flat, flat, rows, rows, rows, flat,
        ),
        check_vma=False,
    )
```

```python
import functools

import jax
import jax.numpy as jnp
from jax import lax
from jax.experimental import pallas as pl
from jax.experimental.pallas import tpu as pltpu
from jax.sharding import PartitionSpec as P

AX = "fsdp"
epsilon = 1e-06
rope_base = 1000000.0
BF = jnp.bfloat16
F32 = jnp.float32
LANES = 128
TILE = 256
STEP_ROWS = 80
GELU_C = 0.7978845608028654
GELU_K = 0.044715
BIG = -1e30


def mm(a, b):
    return lax.dot_general(a, b, (((1,), (0,)), ((), ())), preferred_element_type=F32)


def mm_bt(a, b):
    return lax.dot_general(a, b, (((1,), (1,)), ((), ())), preferred_element_type=F32)


def mm_at(a, b):
    return lax.dot_general(a, b, (((0,), (0,)), ((), ())), preferred_element_type=F32)


def row_mean(v):
    return jnp.mean(v, axis=-1, keepdims=True)


def fold_rows(v):
    return jnp.sum(v.reshape(v.shape[0] // 8, 8, v.shape[1]), axis=0)


def turn(v, cos, sin):
    half = v.shape[1] // 2
    a, b = v[:, :half], v[:, half:]
    return jnp.concatenate([a * cos - b * sin, b * cos + a * sin], axis=1)


def turn_back(v, cos, sin):
    half = v.shape[1] // 2
    a, b = v[:, :half], v[:, half:]
    return jnp.concatenate([a * cos + b * sin, b * cos - a * sin], axis=1)


def norm_back(du, unit, scale):
    return scale * (du - unit * row_mean(du * unit))


def slot_starts(slot, lens_ref, starts_ref):
    first = slot
    inside = jnp.zeros(slot.shape, F32)
    for s in range(lens_ref.shape[0]):
        member = (slot >= starts_ref[s]) & (slot < starts_ref[s] + lens_ref[s])
        first = jnp.where(member, starts_ref[s], first)
        inside = jnp.where(member, 1.0, inside)
    return first, inside


class Pack:
    def __init__(self, chips, narrow, tall, base):
        self.chips = chips
        self.base = base
        self.narrow = narrow
        self.tall = tall
        self.pair = narrow[0][0] // chips
        self.chips_per_step = STEP_ROWS // self.pair
        self.steps = chips // self.chips_per_step
        at = 0
        self.narrow_at = []
        for _, cols in narrow:
            self.narrow_at.append(at)
            at += cols // (2 * LANES) * self.pair
        self.tall_at = []
        for rows, cols in tall:
            self.tall_at.append(at)
            at += cols // LANES * (rows // (2 * chips))
        self.used = at

    def unpack(self, step, ref, narrow_refs, tall_refs):
        rows = slice(self.base, self.base + self.used)
        slabs = [[ref[j, p, rows, :].astype(F32) for p in range(2)] for j in range(self.chips_per_step)]
        at_row = pl.multiple_of(step * STEP_ROWS, 16)
        for (_, cols), start, out in zip(self.narrow, self.narrow_at, narrow_refs):
            tiles = cols // (2 * LANES)
            for p in range(2):
                for t in range(tiles):
                    lo = start + t * self.pair
                    value = jnp.concatenate([s[p][lo : lo + self.pair] for s in slabs], axis=0)
                    col = (p * tiles + t) * LANES
                    out[pl.ds(at_row, STEP_ROWS), col : col + LANES] = value.astype(BF)
        for (rows, cols), start, out in zip(self.tall, self.tall_at, tall_refs):
            own = rows // (2 * self.chips)
            group = self.chips_per_step * 2 * own
            at_tall = pl.multiple_of(step * group, 16)
            for t in range(cols // LANES):
                lo = start + t * own
                value = jnp.concatenate(
                    [s[p][lo : lo + own] for s in slabs for p in range(2)], axis=0
                )
                out[pl.ds(at_tall, group), t * LANES : (t + 1) * LANES] = value.astype(BF)

    def pack(self, step, core, narrow_refs, tall_refs, keep_ref, send_ref):
        at_row = pl.multiple_of(step * STEP_ROWS, 8)
        pieces = [[[] for _ in range(2)] for _ in range(self.chips_per_step)]
        for (_, cols), acc in zip(self.narrow, narrow_refs):
            tiles = cols // (2 * LANES)
            for p in range(2):
                for t in range(tiles):
                    col = (p * tiles + t) * LANES
                    value = acc[pl.ds(at_row, STEP_ROWS), col : col + LANES]
                    for j in range(self.chips_per_step):
                        pieces[j][p].append(value[j * self.pair : (j + 1) * self.pair])
        for (rows, cols), acc in zip(self.tall, tall_refs):
            own = rows // (2 * self.chips)
            group = self.chips_per_step * 2 * own
            at_tall = pl.multiple_of(step * group, 8)
            for t in range(cols // LANES):
                value = acc[pl.ds(at_tall, group), t * LANES : (t + 1) * LANES]
                for j in range(self.chips_per_step):
                    for p in range(2):
                        lo = (2 * j + p) * own
                        pieces[j][p].append(value[lo : lo + own])
        for j in range(self.chips_per_step):
            first = jnp.concatenate(pieces[j][0], axis=0)
            second = jnp.concatenate(pieces[j][1], axis=0)
            keep_ref[j] = jnp.where(core == 0, first, second).astype(BF)
            send_ref[j] = jnp.where(core == 0, second, first).astype(BF)


def forward_kernel(
    pack, heads,
    lens_ref, starts_ref, g_ref, x_ref, cos_ref, sin_ref, gin_ref, gq_ref, gk_ref,
    w_out, h1_ref, qraw_ref, kraw_ref, qn_ref, kn_ref, v_ref, ob_ref,
    w_s, k_s, v_s, bias_s,
):
    step = pl.program_id(0)
    hd = gk_ref.shape[1]
    model = x_ref.shape[1]
    wide = heads * hd

    @pl.when(step < pack.steps)
    def _():
        pack.unpack(step, g_ref, [w_s.at[:, :wide], w_s.at[:, wide : wide + hd], w_s.at[:, wide + hd :]], [])
        w_out[...] = w_s[pl.ds(pl.multiple_of(step * STEP_ROWS, 16), STEP_ROWS), :]

    tile = step - pack.steps

    @pl.when(tile >= 0)
    def _():
        x = x_ref[...].astype(F32)
        scale = lax.rsqrt(row_mean(x * x) + epsilon)
        h1 = (x * scale * gin_ref[...]).astype(BF)
        h1_ref[...] = h1
        cos, sin = cos_ref[...], sin_ref[...]
        raw = mm(h1, w_s[:, :wide])
        qraw_ref[...] = raw
        for h in range(heads):
            part = raw[:, h * hd : (h + 1) * hd]
            unit = part * lax.rsqrt(row_mean(part * part) + epsilon)
            qn_ref[:, h * hd : (h + 1) * hd] = (turn(unit * gq_ref[...], cos, sin) * 0.0625).astype(BF)
        kraw = mm(h1, w_s[:, wide : wide + hd])
        kraw_ref[...] = kraw
        unit = kraw * lax.rsqrt(row_mean(kraw * kraw) + epsilon)
        kn = turn(unit * gk_ref[...], cos, sin).astype(BF)
        kn_ref[...] = kn
        v = mm(h1, w_s[:, wide + hd :]).astype(BF)
        v_ref[...] = v
        at = pl.multiple_of(tile * TILE, TILE)
        k_s[pl.ds(at, TILE), :] = kn
        v_s[pl.ds(at, TILE), :] = v

    for c in range(k_s.shape[0] // TILE):

        @pl.when(tile == c)
        def _():
            span = (c + 1) * TILE
            slot = c * TILE + lax.broadcasted_iota(jnp.int32, (TILE, 1), 0)
            first, _ = slot_starts(slot, lens_ref, starts_ref)
            other = lax.broadcasted_iota(jnp.int32, (TILE, span), 1)
            bias_s[:, :span] = jnp.where((other >= first) & (other <= slot), 0.0, BIG)
            for h in range(heads):
                q = qn_ref[:, h * hd : (h + 1) * hd]
                s = mm_bt(q, k_s[:span, :]) + bias_s[:, :span]
                e = jnp.exp(s - jnp.max(s, axis=-1, keepdims=True))
                inv = 1.0 / jnp.sum(e, axis=-1, keepdims=True)
                o = mm((e * inv).astype(BF), v_s[:span, :])
                ob_ref[:, h * hd : (h + 1) * hd] = o.astype(BF)


def middle_kernel(
    pack, tiles,
    lens_ref, starts_ref, core_ref, g_ref, x_ref, ob_ref, ct_ref, gpost_ref, gpre_ref, gffn_ref,
    res_ref, dx1_ref, dob_ref, dgains_ref, keep_ref, send_ref,
    wg_s, wu_s, wo_s, wd_s, ag_s, au_s, ao_s, ad_s, gain_s,
):
    step = pl.program_id(0)

    @pl.when(step == 0)
    def _():
        for ref in (ag_s, au_s, ao_s, ad_s, gain_s):
            ref[...] = jnp.zeros(ref.shape, F32)

    @pl.when(step < pack.steps)
    def _():
        pack.unpack(step, g_ref, [wg_s, wu_s], [wo_s, wd_s])

    tile = step - pack.steps

    @pl.when((tile >= 0) & (tile < tiles))
    def _():
        slot = tile * TILE + lax.broadcasted_iota(jnp.int32, (TILE, 1), 0)
        _, live = slot_starts(slot, lens_ref, starts_ref)
        ob = ob_ref[...]
        attn = mm(ob, wo_s[...])
        r1 = lax.rsqrt(row_mean(attn * attn) + epsilon)
        na = attn * r1
        x1 = x_ref[...].astype(F32) + na * gpost_ref[...]
        r2 = lax.rsqrt(row_mean(x1 * x1) + epsilon)
        n1 = x1 * r2
        h2 = (n1 * gpre_ref[...]).astype(BF)
        gate = mm(h2, wg_s[...])
        up = mm(h2, wu_s[...])
        th = jnp.tanh(GELU_C * (gate + GELU_K * gate * gate * gate))
        half = 0.5 * (1.0 + th)
        gl = gate * half
        slope = half + 0.5 * gate * (1.0 - th * th) * (GELU_C * (1.0 + 3.0 * GELU_K * gate * gate))
        act = (gl * up).astype(BF)
        f = mm(act, wd_s[...])
        r3 = lax.rsqrt(row_mean(f * f) + epsilon)
        nf = f * r3
        res_ref[...] = (live * (x1 + nf * gffn_ref[...])).astype(BF)
        dy = live * ct_ref[...].astype(F32)
        gain_s[0] += fold_rows(dy * nf)
        df = norm_back(dy * gffn_ref[...], nf, r3).astype(BF)
        dact = mm_bt(df, wd_s[...])
        ad_s[...] += mm_at(act, df)
        dgate = (dact * up * slope).astype(BF)
        dup = (dact * gl).astype(BF)
        ag_s[...] += mm_at(h2, dgate)
        au_s[...] += mm_at(h2, dup)
        dh2 = mm_bt(dgate, wg_s[...]) + mm_bt(dup, wu_s[...])
        gain_s[1] += fold_rows(dh2 * n1)
        dx1 = dy + norm_back(dh2 * gpre_ref[...], n1, r2)
        dx1_ref[...] = dx1
        gain_s[2] += fold_rows(dx1 * na)
        dattn = norm_back(dx1 * gpost_ref[...], na, r1).astype(BF)
        ao_s[...] += mm_at(ob, dattn)
        dob_ref[...] = mm_bt(dattn, wo_s[...]).astype(BF)

    @pl.when(tile >= tiles)
    def _():
        pack.pack(tile - tiles, core_ref[0], [ag_s, au_s], [ao_s, ad_s], keep_ref, send_ref)
        dgains_ref[...] = gain_s[...]


def backward_kernel(
    pack, heads, tiles,
    lens_ref, starts_ref, core_ref, w_ref, x_ref, dx1_ref, h1_ref, qraw_ref, kraw_ref, qn_ref, dob_ref,
    k_ref, v_ref, cos_ref, sin_ref, gin_ref, gq_ref, gk_ref,
    gt_ref, dgin_ref, dgq_ref, dgk_ref, keep_ref, send_ref,
    dq_s, dk_s, dv_s, bias_s, acc_s, dqr_s,
):
    step = pl.program_id(0)
    hd = gk_ref.shape[1]
    wide = heads * hd

    @pl.when(step == 0)
    def _():
        for ref in (dk_s, dv_s, acc_s, dgin_ref, dgq_ref, dgk_ref):
            ref[...] = jnp.zeros(ref.shape, F32)

    for c in range(tiles):

        @pl.when(step == tiles - 1 - c)
        def _():
            span = (c + 1) * TILE
            slot = c * TILE + lax.broadcasted_iota(jnp.int32, (1, TILE), 1)
            first, _ = slot_starts(slot, lens_ref, starts_ref)
            other = lax.broadcasted_iota(jnp.int32, (span, TILE), 0)
            bias_s[:span, :] = jnp.where((other >= first) & (other <= slot), 0.0, BIG)
            for h in range(heads):
                q = qn_ref[:, h * hd : (h + 1) * hd]
                dob = dob_ref[:, h * hd : (h + 1) * hd]
                s = mm_bt(k_ref[:span, :], q) + bias_s[:span, :]
                e = jnp.exp(s - jnp.max(s, axis=0, keepdims=True))
                p = e * (1.0 / jnp.sum(e, axis=0, keepdims=True))
                dv_s[:span, :] += mm(p.astype(BF), dob)
                dp = mm_bt(v_ref[:span, :], dob)
                ds = (p * (dp - jnp.sum(p * dp, axis=0, keepdims=True))).astype(BF)
                dk_s[:span, :] += mm(ds, q)
                dq_s[:, h * hd : (h + 1) * hd] = mm_at(ds, k_ref[:span, :])

    @pl.when(step < tiles)
    def _():
        at = pl.multiple_of((tiles - 1 - step) * TILE, TILE)
        cos, sin = cos_ref[...], sin_ref[...]
        for h in range(heads):
            d = turn_back(dq_s[:, h * hd : (h + 1) * hd], cos, sin) * 0.0625
            part = qraw_ref[:, h * hd : (h + 1) * hd]
            scale = lax.rsqrt(row_mean(part * part) + epsilon)
            unit = part * scale
            dgq_ref[...] += fold_rows(d * unit)
            dqr_s[:, h * hd : (h + 1) * hd] = norm_back(d * gq_ref[...], unit, scale).astype(BF)
        d = turn_back(dk_s[pl.ds(at, TILE), :], cos, sin)
        part = kraw_ref[...]
        scale = lax.rsqrt(row_mean(part * part) + epsilon)
        unit = part * scale
        dgk_ref[...] += fold_rows(d * unit)
        dqr_s[:, wide : wide + hd] = norm_back(d * gk_ref[...], unit, scale).astype(BF)
        dqr_s[:, wide + hd :] = dv_s[pl.ds(at, TILE), :].astype(BF)
        acc_s[...] += mm_at(h1_ref[...], dqr_s[...])
        dh1 = mm_bt(dqr_s[...], w_ref[...])
        x = x_ref[...].astype(F32)
        scale = lax.rsqrt(row_mean(x * x) + epsilon)
        unit = x * scale
        dgin_ref[...] += fold_rows(dh1 * unit)
        gt_ref[...] = dx1_ref[...] + norm_back(dh1 * gin_ref[...], unit, scale)

    @pl.when(step >= tiles)
    def _():
        accs = [acc_s.at[:, :wide], acc_s.at[:, wide : wide + hd], acc_s.at[:, wide + hd :]]
        pack.pack(step - tiles, core_ref[0], accs, [], keep_ref, send_ref)


def smem():
    return pl.BlockSpec(memory_space=pltpu.SMEM)


def whole(shape):
    zeros = (0,) * len(shape)
    return pl.BlockSpec(shape, lambda s: zeros)


def resident(shape):
    zeros = (0,) * len(shape)
    return pl.BlockSpec(shape, lambda s: zeros, pipeline_mode=pl.Buffered(1))


def params(megabytes):
    return pltpu.CompilerParams(
        dimension_semantics=("arbitrary",), vmem_limit_bytes=megabytes * 1024 * 1024
    )


def shape(dims, kind):
    return jax.ShapeDtypeStruct(dims, kind)


def run_forward(pack, heads, lens, starts, gathered, tokens, cos, sin, gin, gq, gk):
    slots, model = tokens.shape
    hd = gk.shape[1]
    wide = heads * hd
    cols = wide + 2 * hd
    last = pack.steps - 1

    def tile_spec(width):
        return pl.BlockSpec((TILE, width), lambda s: (jnp.maximum(s - pack.steps, 0), 0))

    packed = pl.BlockSpec(
        (pack.chips_per_step, 2, gathered.shape[2], LANES), lambda s: (jnp.minimum(s, last), 0, 0, 0)
    )
    return pl.pallas_call(
        functools.partial(forward_kernel, pack, heads),
        grid=(pack.steps + slots // TILE,),
        in_specs=[
            smem(), smem(), packed, tile_spec(model), tile_spec(hd // 2), tile_spec(hd // 2),
            whole((1, model)), whole((1, hd)), whole((1, hd)),
        ],
        out_specs=[
            pl.BlockSpec((STEP_ROWS, cols), lambda s: (jnp.minimum(s, last), 0)),
            tile_spec(model), tile_spec(wide), tile_spec(hd), tile_spec(wide), tile_spec(hd), tile_spec(hd), tile_spec(wide),
        ],
        out_shape=[
            shape((model, cols), BF), shape((slots, model), BF), shape((slots, wide), F32),
            shape((slots, hd), F32), shape((slots, wide), BF), shape((slots, hd), BF), shape((slots, hd), BF),
            shape((slots, wide), BF),
        ],
        scratch_shapes=[
            pltpu.VMEM((model, cols), BF), pltpu.VMEM((slots, hd), BF), pltpu.VMEM((slots, hd), BF),
            pltpu.VMEM((TILE, slots), F32),
        ],
        compiler_params=params(48),
        cost_estimate=pl.CostEstimate(
            flops=2 * slots * model * cols + 4 * slots * slots * wide // 2,
            bytes_accessed=16 * 1024 * 1024, transcendentals=heads * slots * slots,
        ),
        name="attention_forward",
    )(lens, starts, gathered, tokens, cos, sin, gin, gq, gk)


def run_middle(pack, lens, starts, core, gathered, tokens, ob, cotangent, gpost, gpre, gffn):
    slots, model = tokens.shape
    wide = ob.shape[1]
    ff = pack.narrow[0][1]
    tiles = slots // TILE
    last = pack.steps - 1

    def tile_spec(width):
        return pl.BlockSpec((TILE, width), lambda s: (jnp.clip(s - pack.steps, 0, tiles - 1), 0))

    def out_packed():
        return pl.BlockSpec(
            (pack.chips_per_step, pack.used, LANES),
            lambda s: (jnp.maximum(s - pack.steps - tiles, 0), 0, 0),
        )

    packed = pl.BlockSpec(
        (pack.chips_per_step, 2, gathered.shape[2], LANES), lambda s: (jnp.minimum(s, last), 0, 0, 0)
    )
    return pl.pallas_call(
        functools.partial(middle_kernel, pack, tiles),
        grid=(2 * pack.steps + tiles,),
        in_specs=[
            smem(), smem(), smem(), packed, tile_spec(model), tile_spec(wide), tile_spec(model),
            whole((1, model)), whole((1, model)), whole((1, model)),
        ],
        out_specs=[
            tile_spec(model), tile_spec(model), tile_spec(wide), whole((3, 8, model)), out_packed(), out_packed(),
        ],
        out_shape=[
            shape((slots, model), BF), shape((slots, model), F32), shape((slots, wide), BF),
            shape((3, 8, model), F32),
            shape((pack.chips, pack.used, LANES), BF), shape((pack.chips, pack.used, LANES), BF),
        ],
        scratch_shapes=[
            pltpu.VMEM((model, ff), BF), pltpu.VMEM((model, ff), BF), pltpu.VMEM((wide, model), BF),
            pltpu.VMEM((ff, model), BF),
            pltpu.VMEM((model, ff), F32), pltpu.VMEM((model, ff), F32), pltpu.VMEM((wide, model), F32),
            pltpu.VMEM((ff, model), F32), pltpu.VMEM((3, 8, model), F32),
        ],
        compiler_params=params(60),
        cost_estimate=pl.CostEstimate(
            flops=6 * slots * model * (3 * ff + wide), bytes_accessed=36 * 1024 * 1024,
            transcendentals=slots * ff,
        ),
        name="output_and_ffn",
    )(lens, starts, core, gathered, tokens, ob, cotangent, gpost, gpre, gffn)


def run_backward(pack, heads, lens, starts, core, weights, tokens, dx1, h1, qraw, kraw, qn, dob, kn, v, cos, sin, gin, gq, gk):
    slots, model = tokens.shape
    hd = gk.shape[1]
    wide = heads * hd
    cols = wide + 2 * hd
    tiles = slots // TILE

    def tile_spec(width):
        return pl.BlockSpec((TILE, width), lambda s: (jnp.maximum(tiles - 1 - s, 0), 0))

    def out_packed():
        return pl.BlockSpec(
            (pack.chips_per_step, pack.used, LANES), lambda s: (jnp.maximum(s - tiles, 0), 0, 0)
        )

    return pl.pallas_call(
        functools.partial(backward_kernel, pack, heads, tiles),
        grid=(tiles + pack.steps,),
        in_specs=[
            smem(), smem(), smem(), resident((model, cols)), tile_spec(model), tile_spec(model), tile_spec(model),
            tile_spec(wide), tile_spec(hd), tile_spec(wide), tile_spec(wide), resident((slots, hd)), resident((slots, hd)),
            tile_spec(hd // 2), tile_spec(hd // 2), whole((1, model)), whole((1, hd)), whole((1, hd)),
        ],
        out_specs=[
            tile_spec(model), whole((8, model)), whole((8, hd)), whole((8, hd)), out_packed(), out_packed(),
        ],
        out_shape=[
            shape((slots, model), F32), shape((8, model), F32), shape((8, hd), F32), shape((8, hd), F32),
            shape((pack.chips, pack.used, LANES), BF), shape((pack.chips, pack.used, LANES), BF),
        ],
        scratch_shapes=[
            pltpu.VMEM((TILE, wide), F32), pltpu.VMEM((slots, hd), F32), pltpu.VMEM((slots, hd), F32),
            pltpu.VMEM((slots, TILE), F32), pltpu.VMEM((model, cols), F32), pltpu.VMEM((TILE, cols), BF),
        ],
        compiler_params=params(56),
        cost_estimate=pl.CostEstimate(
            flops=4 * slots * model * cols + 10 * slots * slots * wide // 2,
            bytes_accessed=24 * 1024 * 1024, transcendentals=heads * slots * slots,
        ),
        name="attention_backward",
    )(lens, starts, core, weights, tokens, dx1, h1, qraw, kraw, qn, dob, kn, v, cos, sin, gin, gq, gk)


class Mover:
    def __init__(self, device_count):
        self.n = device_count
        self.chips = device_count // 2
        self.digits = 0
        while 4 ** (self.digits + 1) <= self.chips:
            self.digits += 1
        me = lax.axis_index(AX)
        self.core = me % 2
        self.chip = me // 2

    def swap(self, value, mask=1):
        return lax.ppermute(value, AX, [(i, i ^ mask) for i in range(self.n)])

    def in_core_order(self, mine, other):
        first = self.core == 0
        return jnp.where(first, mine, other), jnp.where(first, other, mine)

    def trade_halves(self, narrow):
        halves = [jnp.split(w, 2, axis=1) for w in narrow]
        low = jnp.concatenate([h[0] for h in halves], axis=1)
        high = jnp.concatenate([h[1] for h in halves], axis=1)
        first = self.core == 0
        mine = jnp.where(first, low, high)
        other = self.swap(jnp.where(first, high, low))
        return jnp.concatenate(self.in_core_order(mine, other), axis=0)

    def gather(self, blocks):
        tiles = [b.reshape(b.shape[0], -1, LANES).transpose(1, 0, 2).reshape(-1, LANES) for b in blocks]
        whole_array = lax.all_gather(jnp.concatenate(tiles, axis=0), AX, axis=0)
        return whole_array.reshape(self.chips, 2, -1, LANES)

    def cores(self, keep, send):
        return keep.astype(F32) + self.swap(send).astype(F32)

    def digit(self, total, digit):
        low = total.astype(BF).reshape(total.shape[0] // 4, 4, -1, LANES)
        here = (self.chip >> (2 * digit)) % 4
        moved = [
            self.swap(
                lax.dynamic_index_in_dim(low, here ^ j, 1, keepdims=False), j << (2 * digit + 1)
            )
            for j in (1, 2, 3)
        ]
        total = lax.dynamic_index_in_dim(total.reshape(low.shape), here, 1, keepdims=False)
        for m in moved:
            total = total + m.astype(F32)
        return total

    def split_narrow(self, total, pack):
        rows = pack.pair // 2
        count = sum(cols // (2 * LANES) for _, cols in pack.narrow)
        tiles = total[: count * pack.pair].reshape(-1, 2, rows, LANES)
        mine = lax.dynamic_index_in_dim(tiles, self.core, 1, keepdims=False)
        other = self.swap(lax.dynamic_index_in_dim(tiles, 1 - self.core, 1, keepdims=False))
        halves = self.in_core_order(mine, other)
        outs, at = [], 0
        for _, cols in pack.narrow:
            t = cols // (2 * LANES)
            both = jnp.stack([h[at : at + t] for h in halves])
            outs.append(both.transpose(2, 0, 1, 3).reshape(rows, cols))
            at += t
        return outs

    def split_tall(self, total, pack):
        outs = []
        for (rows, cols), at in zip(pack.tall, pack.tall_at):
            own, t = rows // self.n, cols // LANES
            piece = total[at : at + t * own].reshape(t, own, LANES)
            outs.append(piece.transpose(1, 0, 2).reshape(own, cols))
        return outs


def on_device(
    device_count,
    tokens,
    cotangent,
    seq_lens,
    seq_starts,
    input_gain,
    w_query,
    w_key,
    w_value,
    query_gain,
    key_gain,
    w_output,
    attn_post_gain,
    ffn_pre_gain,
    w_gate,
    w_up,
    w_down,
    ffn_post_gain,
):
    mover = Mover(device_count)
    chips = mover.chips
    slots, model = tokens.shape
    hd = w_key.shape[1]
    heads = w_query.shape[1] // hd
    ffn = Pack(
        chips,
        [(model, w_gate.shape[1]), (model, w_up.shape[1])],
        [(w_output.shape[0] * device_count, model), (w_down.shape[0] * device_count, model)],
        0,
    )
    attn = Pack(chips, [(model, heads * hd), (model, hd), (model, hd)], [], ffn.used)

    gains = [input_gain, query_gain, key_gain, attn_post_gain, ffn_pre_gain, ffn_post_gain]
    flat = jnp.concatenate(gains)
    flat = jnp.pad(flat, (0, 8 * LANES - flat.shape[0])).reshape(8, LANES)
    narrow = mover.trade_halves([w_gate, w_up, w_query, w_key, w_value])
    split = w_gate.shape[1]
    gathered = mover.gather([narrow[:, :split], w_output, w_down, narrow[:, split:], flat])
    flat = gathered[:, :, ffn.used + attn.used :].reshape(device_count, 8 * LANES)
    vectors, at = [], 0
    for g in gains:
        vectors.append(flat[:, at : at + g.shape[0]].reshape(1, -1).astype(F32))
        at += g.shape[0]
    gin, gq, gk, gpost, gpre, gffn = vectors

    slot = jnp.arange(slots, dtype=jnp.int32)
    inside = (slot[None, :] >= seq_starts[:, None]) & (
        slot[None, :] < seq_starts[:, None] + seq_lens[:, None]
    )
    offset = jnp.sum(jnp.where(inside, seq_starts[:, None], 0), axis=0)
    frequency = rope_base ** (-2.0 * jnp.arange(hd // 2, dtype=F32) / hd)
    angles = (slot - offset).astype(F32)[:, None] * frequency[None, :]
    cos, sin = jnp.cos(angles), jnp.sin(angles)
    core = mover.core.astype(jnp.int32).reshape(1)

    weights, h1, qraw, kraw, qn, kn, v, ob = run_forward(
        attn, heads, seq_lens, seq_starts, gathered, tokens, cos, sin, gin, gq, gk
    )
    result, dx1, dob, dgains, keep, send = run_middle(
        ffn, seq_lens, seq_starts, core, gathered, tokens, ob, cotangent, gpost, gpre, gffn
    )
    ffn_sum = mover.cores(keep, send)
    dob, ffn_sum = lax.optimization_barrier((dob, ffn_sum))
    grad_tokens, dgin, dgq, dgk, keep, send = run_backward(
        attn, heads, seq_lens, seq_starts, core, weights, tokens, dx1, h1, qraw, kraw, qn, dob, kn, v,
        cos, sin, gin, gq, gk,
    )
    dffn, dpre, dpost = (jnp.sum(dgains[i], axis=0) for i in range(3))
    grads = [jnp.sum(dgin, axis=0), jnp.sum(dgq, axis=0), jnp.sum(dgk, axis=0), dpost, dpre, dffn]
    flat = jnp.concatenate([g.reshape(device_count, -1) for g in grads], axis=1).astype(BF)
    flat = jnp.pad(flat, ((0, 0), (0, 8 * LANES - flat.shape[1]))).reshape(chips, 2, 8, LANES)
    keep = jnp.concatenate(
        [keep, lax.dynamic_index_in_dim(flat, mover.core, 1, keepdims=False)], axis=1
    )
    send = jnp.concatenate(
        [send, lax.dynamic_index_in_dim(flat, 1 - mover.core, 1, keepdims=False)], axis=1
    )
    attn_sum = mover.cores(keep, send)
    for d in range(mover.digits):
        ffn_sum = mover.digit(ffn_sum, d)
        attn_sum = mover.digit(attn_sum, d)
    ffn_sum, attn_sum = ffn_sum[0], attn_sum[0]
    own_gate, own_up = mover.split_narrow(ffn_sum, ffn)
    own_output, own_down = mover.split_tall(ffn_sum, ffn)
    own_query, own_key, own_value = mover.split_narrow(attn_sum, attn)
    flat = attn_sum[attn.used :].reshape(-1)
    owned, at = [], 0
    for g in gains:
        owned.append(flat[at : at + g.shape[0]])
        at += g.shape[0]
    own_gin, own_gq, own_gk, own_gpost, own_gpre, own_gffn = owned
    return (
        result, grad_tokens, own_gin, own_query, own_key, own_value, own_gq, own_gk, own_output, own_gpost,
        own_gpre, own_gate, own_up, own_down, own_gffn,
    )


def solution(mesh):
    rows, flat = P(AX, None), P(AX)
    device_count = mesh.shape[AX]

    def block(*arrays):
        return on_device(device_count, *arrays)

    return jax.shard_map(
        block,
        mesh=mesh,
        in_specs=(
            rows, rows, flat, flat, flat, rows, rows, rows, flat, flat, rows, flat, flat, rows, rows, rows, flat,
        ),
        out_specs=(
            rows, rows, flat, rows, rows, rows, flat, flat, rows, flat, flat, rows, rows, rows, flat,
        ),
        check_vma=False,
    )
```

```python
import functools

import jax
import jax.numpy as jnp
from jax import lax
from jax.experimental import pallas as pl
from jax.experimental.pallas import tpu as pltpu
from jax.sharding import PartitionSpec as P

AX = "fsdp"
epsilon = 1e-06
rope_base = 1000000.0
BF = jnp.bfloat16
F32 = jnp.float32
LANES = 128
TILE = 256
STEP_ROWS = 80
GELU_C = 0.7978845608028654
GELU_K = 0.044715
BIG = -1e30


def mm(a, b):
    return lax.dot_general(a, b, (((1,), (0,)), ((), ())), preferred_element_type=F32)


def mm_bt(a, b):
    return lax.dot_general(a, b, (((1,), (1,)), ((), ())), preferred_element_type=F32)


def mm_at(a, b):
    return lax.dot_general(a, b, (((0,), (0,)), ((), ())), preferred_element_type=F32)


def row_mean(v):
    return jnp.mean(v, axis=-1, keepdims=True)


def fold_rows(v):
    return jnp.sum(v.reshape(v.shape[0] // 8, 8, v.shape[1]), axis=0)


def turn(v, cos, sin):
    half = v.shape[1] // 2
    a, b = v[:, :half], v[:, half:]
    return jnp.concatenate([a * cos - b * sin, b * cos + a * sin], axis=1)


def turn_back(v, cos, sin):
    half = v.shape[1] // 2
    a, b = v[:, :half], v[:, half:]
    return jnp.concatenate([a * cos + b * sin, b * cos - a * sin], axis=1)


def norm_back(du, unit, scale):
    return scale * (du - unit * row_mean(du * unit))


def slot_starts(slot, lens_ref, starts_ref):
    first = slot
    inside = jnp.zeros(slot.shape, F32)
    for s in range(lens_ref.shape[0]):
        member = (slot >= starts_ref[s]) & (slot < starts_ref[s] + lens_ref[s])
        first = jnp.where(member, starts_ref[s], first)
        inside = jnp.where(member, 1.0, inside)
    return first, inside


class Pack:
    def __init__(self, chips, narrow, tall):
        self.chips = chips
        self.narrow = narrow
        self.tall = tall
        self.pair = narrow[0][0] // chips
        self.chips_per_step = STEP_ROWS // self.pair
        self.steps = chips // self.chips_per_step
        at = 0
        self.narrow_at = []
        for _, cols in narrow:
            self.narrow_at.append(at)
            at += cols // (2 * LANES) * self.pair
        self.tall_at = []
        for rows, cols in tall:
            self.tall_at.append(at)
            at += cols // LANES * (rows // (2 * chips))
        self.used = at

    def unpack(self, step, slabs, narrow_refs, tall_refs):
        slabs = [[value[: self.used].astype(F32) for value in pair] for pair in slabs]
        at_row = pl.multiple_of(step * STEP_ROWS, 16)
        for (_, cols), start, out in zip(self.narrow, self.narrow_at, narrow_refs):
            tiles = cols // (2 * LANES)
            for p in range(2):
                for t in range(tiles):
                    lo = start + t * self.pair
                    value = jnp.concatenate([s[p][lo : lo + self.pair] for s in slabs], axis=0)
                    col = (p * tiles + t) * LANES
                    out[pl.ds(at_row, STEP_ROWS), col : col + LANES] = value.astype(BF)
        for (rows, cols), start, out in zip(self.tall, self.tall_at, tall_refs):
            own = rows // (2 * self.chips)
            group = self.chips_per_step * 2 * own
            at_tall = pl.multiple_of(step * group, 16)
            for t in range(cols // LANES):
                lo = start + t * own
                value = jnp.concatenate(
                    [s[p][lo : lo + own] for s in slabs for p in range(2)], axis=0
                )
                out[pl.ds(at_tall, group), t * LANES : (t + 1) * LANES] = value.astype(BF)

    def pack(self, step, core, narrow_refs, tall_refs, keep_ref, send_ref):
        at_row = pl.multiple_of(step * STEP_ROWS, 8)
        pieces = [[[] for _ in range(2)] for _ in range(self.chips_per_step)]
        for (_, cols), acc in zip(self.narrow, narrow_refs):
            tiles = cols // (2 * LANES)
            for p in range(2):
                for t in range(tiles):
                    col = (p * tiles + t) * LANES
                    value = acc[pl.ds(at_row, STEP_ROWS), col : col + LANES]
                    for j in range(self.chips_per_step):
                        pieces[j][p].append(value[j * self.pair : (j + 1) * self.pair])
        for (rows, cols), acc in zip(self.tall, tall_refs):
            own = rows // (2 * self.chips)
            group = self.chips_per_step * 2 * own
            at_tall = pl.multiple_of(step * group, 8)
            for t in range(cols // LANES):
                value = acc[pl.ds(at_tall, group), t * LANES : (t + 1) * LANES]
                for j in range(self.chips_per_step):
                    for p in range(2):
                        lo = (2 * j + p) * own
                        pieces[j][p].append(value[lo : lo + own])
        for j in range(self.chips_per_step):
            first = jnp.concatenate(pieces[j][0], axis=0)
            second = jnp.concatenate(pieces[j][1], axis=0)
            keep_ref[j] = jnp.where(core == 0, first, second).astype(BF)
            send_ref[j] = jnp.where(core == 0, second, first).astype(BF)


def forward_kernel(
    pack, heads,
    lens_ref, starts_ref, place_ref, *refs,
):
    count = pack.chips_per_step
    mine_refs, other_refs, refs = refs[:count], refs[count : 2 * count], refs[2 * count :]
    (
        x_ref, cos_ref, sin_ref, gin_ref, gq_ref, gk_ref,
        w_out, h1_ref, qraw_ref, kraw_ref, qn_ref, kn_ref, v_ref, ob_ref,
        w_s, k_s, v_s, bias_s,
    ) = refs
    step = pl.program_id(0)
    hd = gk_ref.shape[1]
    model = x_ref.shape[1]
    wide = heads * hd

    @pl.when(step < pack.steps)
    def _():
        first = place_ref[0] == 0
        slabs = []
        for mine_ref, other_ref in zip(mine_refs, other_refs):
            mine, other = mine_ref[0].astype(F32), other_ref[0].astype(F32)
            slabs.append([jnp.where(first, mine, other), jnp.where(first, other, mine)])
        pack.unpack(step, slabs, [w_s.at[:, :wide], w_s.at[:, wide : wide + hd], w_s.at[:, wide + hd :]], [])
        w_out[...] = w_s[pl.ds(pl.multiple_of(step * STEP_ROWS, 16), STEP_ROWS), :]

    tile = step - pack.steps

    @pl.when(tile >= 0)
    def _():
        x = x_ref[...].astype(F32)
        scale = lax.rsqrt(row_mean(x * x) + epsilon)
        h1 = (x * scale * gin_ref[...]).astype(BF)
        h1_ref[...] = h1
        cos, sin = cos_ref[...], sin_ref[...]
        raw = mm(h1, w_s[:, :wide])
        qraw_ref[...] = raw
        for h in range(heads):
            part = raw[:, h * hd : (h + 1) * hd]
            unit = part * lax.rsqrt(row_mean(part * part) + epsilon)
            qn_ref[:, h * hd : (h + 1) * hd] = (turn(unit * gq_ref[...], cos, sin) * 0.0625).astype(BF)
        kraw = mm(h1, w_s[:, wide : wide + hd])
        kraw_ref[...] = kraw
        unit = kraw * lax.rsqrt(row_mean(kraw * kraw) + epsilon)
        kn = turn(unit * gk_ref[...], cos, sin).astype(BF)
        kn_ref[...] = kn
        v = mm(h1, w_s[:, wide + hd :]).astype(BF)
        v_ref[...] = v
        at = pl.multiple_of(tile * TILE, TILE)
        k_s[pl.ds(at, TILE), :] = kn
        v_s[pl.ds(at, TILE), :] = v

    for c in range(k_s.shape[0] // TILE):

        @pl.when(tile == c)
        def _():
            span = (c + 1) * TILE
            slot = c * TILE + lax.broadcasted_iota(jnp.int32, (TILE, 1), 0)
            first, _ = slot_starts(slot, lens_ref, starts_ref)
            other = lax.broadcasted_iota(jnp.int32, (TILE, span), 1)
            bias_s[:, :span] = jnp.where((other >= first) & (other <= slot), 0.0, BIG)
            for h in range(heads):
                q = qn_ref[:, h * hd : (h + 1) * hd]
                s = mm_bt(q, k_s[:span, :]) + bias_s[:, :span]
                e = jnp.exp(s - jnp.max(s, axis=-1, keepdims=True))
                inv = 1.0 / jnp.sum(e, axis=-1, keepdims=True)
                o = mm((e * inv).astype(BF), v_s[:span, :])
                ob_ref[:, h * hd : (h + 1) * hd] = o.astype(BF)


def middle_kernel(
    pack, tiles,
    lens_ref, starts_ref, core_ref, g_ref, x_ref, ob_ref, ct_ref, gpost_ref, gpre_ref, gffn_ref,
    res_ref, dx1_ref, dob_ref, dgains_ref, keep_ref, send_ref,
    wg_s, wu_s, wo_s, wd_s, ag_s, au_s, ao_s, ad_s, gain_s,
):
    step = pl.program_id(0)

    @pl.when(step == 0)
    def _():
        for ref in (ag_s, au_s, ao_s, ad_s, gain_s):
            ref[...] = jnp.zeros(ref.shape, F32)

    @pl.when(step < pack.steps)
    def _():
        slabs = [[g_ref[j, p] for p in range(2)] for j in range(pack.chips_per_step)]
        pack.unpack(step, slabs, [wg_s, wu_s], [wo_s, wd_s])

    tile = step - pack.steps

    @pl.when((tile >= 0) & (tile < tiles))
    def _():
        slot = tile * TILE + lax.broadcasted_iota(jnp.int32, (TILE, 1), 0)
        _, live = slot_starts(slot, lens_ref, starts_ref)
        ob = ob_ref[...]
        attn = mm(ob, wo_s[...])
        r1 = lax.rsqrt(row_mean(attn * attn) + epsilon)
        na = attn * r1
        x1 = x_ref[...].astype(F32) + na * gpost_ref[...]
        r2 = lax.rsqrt(row_mean(x1 * x1) + epsilon)
        n1 = x1 * r2
        h2 = (n1 * gpre_ref[...]).astype(BF)
        gate = mm(h2, wg_s[...])
        up = mm(h2, wu_s[...])
        th = jnp.tanh(GELU_C * (gate + GELU_K * gate * gate * gate))
        half = 0.5 * (1.0 + th)
        gl = gate * half
        slope = half + 0.5 * gate * (1.0 - th * th) * (GELU_C * (1.0 + 3.0 * GELU_K * gate * gate))
        act = (gl * up).astype(BF)
        f = mm(act, wd_s[...])
        r3 = lax.rsqrt(row_mean(f * f) + epsilon)
        nf = f * r3
        res_ref[...] = (live * (x1 + nf * gffn_ref[...])).astype(BF)
        dy = live * ct_ref[...].astype(F32)
        gain_s[0] += fold_rows(dy * nf)
        df = norm_back(dy * gffn_ref[...], nf, r3).astype(BF)
        dact = mm_bt(df, wd_s[...])
        ad_s[...] += mm_at(act, df)
        dgate = (dact * up * slope).astype(BF)
        dup = (dact * gl).astype(BF)
        ag_s[...] += mm_at(h2, dgate)
        au_s[...] += mm_at(h2, dup)
        dh2 = mm_bt(dgate, wg_s[...]) + mm_bt(dup, wu_s[...])
        gain_s[1] += fold_rows(dh2 * n1)
        dx1 = dy + norm_back(dh2 * gpre_ref[...], n1, r2)
        dx1_ref[...] = dx1
        gain_s[2] += fold_rows(dx1 * na)
        dattn = norm_back(dx1 * gpost_ref[...], na, r1).astype(BF)
        ao_s[...] += mm_at(ob, dattn)
        dob_ref[...] = mm_bt(dattn, wo_s[...]).astype(BF)

    @pl.when(tile >= tiles)
    def _():
        pack.pack(tile - tiles, core_ref[0], [ag_s, au_s], [ao_s, ad_s], keep_ref, send_ref)
        dgains_ref[...] = gain_s[...]


def backward_kernel(
    pack, heads, tiles,
    lens_ref, starts_ref, core_ref, w_ref, x_ref, dx1_ref, h1_ref, qraw_ref, kraw_ref, qn_ref, dob_ref,
    k_ref, v_ref, cos_ref, sin_ref, gin_ref, gq_ref, gk_ref,
    gt_ref, dgin_ref, dgq_ref, dgk_ref, keep_ref, send_ref,
    dq_s, dk_s, dv_s, bias_s, acc_s, dqr_s,
):
    step = pl.program_id(0)
    hd = gk_ref.shape[1]
    wide = heads * hd

    @pl.when(step == 0)
    def _():
        for ref in (dk_s, dv_s, acc_s, dgin_ref, dgq_ref, dgk_ref):
            ref[...] = jnp.zeros(ref.shape, F32)

    for c in range(tiles):

        @pl.when(step == tiles - 1 - c)
        def _():
            span = (c + 1) * TILE
            slot = c * TILE + lax.broadcasted_iota(jnp.int32, (1, TILE), 1)
            first, _ = slot_starts(slot, lens_ref, starts_ref)
            other = lax.broadcasted_iota(jnp.int32, (span, TILE), 0)
            bias_s[:span, :] = jnp.where((other >= first) & (other <= slot), 0.0, BIG)
            for h in range(heads):
                q = qn_ref[:, h * hd : (h + 1) * hd]
                dob = dob_ref[:, h * hd : (h + 1) * hd]
                s = mm_bt(k_ref[:span, :], q) + bias_s[:span, :]
                e = jnp.exp(s - jnp.max(s, axis=0, keepdims=True))
                p = e * (1.0 / jnp.sum(e, axis=0, keepdims=True))
                dv_s[:span, :] += mm(p.astype(BF), dob)
                dp = mm_bt(v_ref[:span, :], dob)
                ds = (p * (dp - jnp.sum(p * dp, axis=0, keepdims=True))).astype(BF)
                dk_s[:span, :] += mm(ds, q)
                dq_s[:, h * hd : (h + 1) * hd] = mm_at(ds, k_ref[:span, :])

    @pl.when(step < tiles)
    def _():
        at = pl.multiple_of((tiles - 1 - step) * TILE, TILE)
        cos, sin = cos_ref[...], sin_ref[...]
        for h in range(heads):
            d = turn_back(dq_s[:, h * hd : (h + 1) * hd], cos, sin) * 0.0625
            part = qraw_ref[:, h * hd : (h + 1) * hd]
            scale = lax.rsqrt(row_mean(part * part) + epsilon)
            unit = part * scale
            dgq_ref[...] += fold_rows(d * unit)
            dqr_s[:, h * hd : (h + 1) * hd] = norm_back(d * gq_ref[...], unit, scale).astype(BF)
        d = turn_back(dk_s[pl.ds(at, TILE), :], cos, sin)
        part = kraw_ref[...]
        scale = lax.rsqrt(row_mean(part * part) + epsilon)
        unit = part * scale
        dgk_ref[...] += fold_rows(d * unit)
        dqr_s[:, wide : wide + hd] = norm_back(d * gk_ref[...], unit, scale).astype(BF)
        dqr_s[:, wide + hd :] = dv_s[pl.ds(at, TILE), :].astype(BF)
        acc_s[...] += mm_at(h1_ref[...], dqr_s[...])
        dh1 = mm_bt(dqr_s[...], w_ref[...])
        x = x_ref[...].astype(F32)
        scale = lax.rsqrt(row_mean(x * x) + epsilon)
        unit = x * scale
        dgin_ref[...] += fold_rows(dh1 * unit)
        gt_ref[...] = dx1_ref[...] + norm_back(dh1 * gin_ref[...], unit, scale)

    @pl.when(step >= tiles)
    def _():
        accs = [acc_s.at[:, :wide], acc_s.at[:, wide : wide + hd], acc_s.at[:, wide + hd :]]
        pack.pack(step - tiles, core_ref[0], accs, [], keep_ref, send_ref)


def smem():
    return pl.BlockSpec(memory_space=pltpu.SMEM)


def whole(shape):
    zeros = (0,) * len(shape)
    return pl.BlockSpec(shape, lambda s: zeros)


def resident(shape):
    zeros = (0,) * len(shape)
    return pl.BlockSpec(shape, lambda s: zeros, pipeline_mode=pl.Buffered(1))


def params(megabytes):
    return pltpu.CompilerParams(
        dimension_semantics=("arbitrary",), vmem_limit_bytes=megabytes * 1024 * 1024
    )


def shape(dims, kind):
    return jax.ShapeDtypeStruct(dims, kind)


def run_forward(pack, heads, lens, starts, place, mine, other, tokens, cos, sin, gin, gq, gk):
    slots, model = tokens.shape
    hd = gk.shape[1]
    wide = heads * hd
    cols = wide + 2 * hd
    last = pack.steps - 1
    count = pack.chips_per_step

    def tile_spec(width):
        return pl.BlockSpec((TILE, width), lambda s, *_: (jnp.maximum(s - pack.steps, 0), 0))

    def fixed(width):
        return pl.BlockSpec((1, width), lambda s, *_: (0, 0))

    def slab(j):
        def index(s, lens_ref, starts_ref, place_ref):
            far = (jnp.minimum(s, last) * count + j) ^ place_ref[1]
            turned = jnp.int32(0)
            left = pack.chips
            while left > 1:
                turned = turned * 4 + far % 4
                far, left = far // 4, left // 4
            return turned, 0, 0

        return pl.BlockSpec((1, mine.shape[1], LANES), index)

    return pl.pallas_call(
        functools.partial(forward_kernel, pack, heads),
        grid_spec=pltpu.PrefetchScalarGridSpec(
            num_scalar_prefetch=3,
            grid=(pack.steps + slots // TILE,),
            in_specs=[slab(j) for j in range(count)] * 2
            + [tile_spec(model), tile_spec(hd // 2), tile_spec(hd // 2), fixed(model), fixed(hd), fixed(hd)],
            out_specs=[
                pl.BlockSpec((STEP_ROWS, cols), lambda s, *_: (jnp.minimum(s, last), 0)),
                tile_spec(model), tile_spec(wide), tile_spec(hd), tile_spec(wide), tile_spec(hd), tile_spec(hd),
                tile_spec(wide),
            ],
            scratch_shapes=[
                pltpu.VMEM((model, cols), BF), pltpu.VMEM((slots, hd), BF), pltpu.VMEM((slots, hd), BF),
                pltpu.VMEM((TILE, slots), F32),
            ],
        ),
        out_shape=[
            shape((model, cols), BF), shape((slots, model), BF), shape((slots, wide), F32),
            shape((slots, hd), F32), shape((slots, wide), BF), shape((slots, hd), BF), shape((slots, hd), BF),
            shape((slots, wide), BF),
        ],
        compiler_params=params(48),
        cost_estimate=pl.CostEstimate(
            flops=2 * slots * model * cols + 4 * slots * slots * wide // 2,
            bytes_accessed=16 * 1024 * 1024, transcendentals=heads * slots * slots,
        ),
        name="attention_forward",
    )(lens, starts, place, *([mine] * count), *([other] * count), tokens, cos, sin, gin, gq, gk)


def run_middle(pack, lens, starts, core, gathered, tokens, ob, cotangent, gpost, gpre, gffn):
    slots, model = tokens.shape
    wide = ob.shape[1]
    ff = pack.narrow[0][1]
    tiles = slots // TILE
    last = pack.steps - 1

    def tile_spec(width):
        return pl.BlockSpec((TILE, width), lambda s: (jnp.clip(s - pack.steps, 0, tiles - 1), 0))

    def out_packed():
        return pl.BlockSpec(
            (pack.chips_per_step, pack.used, LANES),
            lambda s: (jnp.maximum(s - pack.steps - tiles, 0), 0, 0),
        )

    packed = pl.BlockSpec(
        (pack.chips_per_step, 2, gathered.shape[2], LANES), lambda s: (jnp.minimum(s, last), 0, 0, 0)
    )
    return pl.pallas_call(
        functools.partial(middle_kernel, pack, tiles),
        grid=(2 * pack.steps + tiles,),
        in_specs=[
            smem(), smem(), smem(), packed, tile_spec(model), tile_spec(wide), tile_spec(model),
            whole((1, model)), whole((1, model)), whole((1, model)),
        ],
        out_specs=[
            tile_spec(model), tile_spec(model), tile_spec(wide), whole((3, 8, model)), out_packed(), out_packed(),
        ],
        out_shape=[
            shape((slots, model), BF), shape((slots, model), F32), shape((slots, wide), BF),
            shape((3, 8, model), F32),
            shape((pack.chips, pack.used, LANES), BF), shape((pack.chips, pack.used, LANES), BF),
        ],
        scratch_shapes=[
            pltpu.VMEM((model, ff), BF), pltpu.VMEM((model, ff), BF), pltpu.VMEM((wide, model), BF),
            pltpu.VMEM((ff, model), BF),
            pltpu.VMEM((model, ff), F32), pltpu.VMEM((model, ff), F32), pltpu.VMEM((wide, model), F32),
            pltpu.VMEM((ff, model), F32), pltpu.VMEM((3, 8, model), F32),
        ],
        compiler_params=params(60),
        cost_estimate=pl.CostEstimate(
            flops=6 * slots * model * (3 * ff + wide), bytes_accessed=36 * 1024 * 1024,
            transcendentals=slots * ff,
        ),
        name="output_and_ffn",
    )(lens, starts, core, gathered, tokens, ob, cotangent, gpost, gpre, gffn)


def run_backward(pack, heads, lens, starts, core, weights, tokens, dx1, h1, qraw, kraw, qn, dob, kn, v, cos, sin, gin, gq, gk):
    slots, model = tokens.shape
    hd = gk.shape[1]
    wide = heads * hd
    cols = wide + 2 * hd
    tiles = slots // TILE

    def tile_spec(width):
        return pl.BlockSpec((TILE, width), lambda s: (jnp.maximum(tiles - 1 - s, 0), 0))

    def out_packed():
        return pl.BlockSpec(
            (pack.chips_per_step, pack.used, LANES), lambda s: (jnp.maximum(s - tiles, 0), 0, 0)
        )

    return pl.pallas_call(
        functools.partial(backward_kernel, pack, heads, tiles),
        grid=(tiles + pack.steps,),
        in_specs=[
            smem(), smem(), smem(), resident((model, cols)), tile_spec(model), tile_spec(model), tile_spec(model),
            tile_spec(wide), tile_spec(hd), tile_spec(wide), tile_spec(wide), resident((slots, hd)), resident((slots, hd)),
            tile_spec(hd // 2), tile_spec(hd // 2), whole((1, model)), whole((1, hd)), whole((1, hd)),
        ],
        out_specs=[
            tile_spec(model), whole((8, model)), whole((8, hd)), whole((8, hd)), out_packed(), out_packed(),
        ],
        out_shape=[
            shape((slots, model), F32), shape((8, model), F32), shape((8, hd), F32), shape((8, hd), F32),
            shape((pack.chips, pack.used, LANES), BF), shape((pack.chips, pack.used, LANES), BF),
        ],
        scratch_shapes=[
            pltpu.VMEM((TILE, wide), F32), pltpu.VMEM((slots, hd), F32), pltpu.VMEM((slots, hd), F32),
            pltpu.VMEM((slots, TILE), F32), pltpu.VMEM((model, cols), F32), pltpu.VMEM((TILE, cols), BF),
        ],
        compiler_params=params(56),
        cost_estimate=pl.CostEstimate(
            flops=4 * slots * model * cols + 10 * slots * slots * wide // 2,
            bytes_accessed=24 * 1024 * 1024, transcendentals=heads * slots * slots,
        ),
        name="attention_backward",
    )(lens, starts, core, weights, tokens, dx1, h1, qraw, kraw, qn, dob, kn, v, cos, sin, gin, gq, gk)


def format_base4(value, digits):
    return [str((value >> (2 * d)) % 4) for d in reversed(range(digits))]


class Mover:
    def __init__(self, device_count):
        self.n = device_count
        self.chips = device_count // 2
        self.digits = 0
        while 4 ** (self.digits + 1) <= self.chips:
            self.digits += 1
        me = lax.axis_index(AX)
        self.core = me % 2
        self.chip = me // 2

    def swap(self, value, mask=1):
        return lax.ppermute(value, AX, [(i, i ^ mask) for i in range(self.n)])

    def in_core_order(self, mine, other):
        first = self.core == 0
        return jnp.where(first, mine, other), jnp.where(first, other, mine)

    def trade_halves(self, narrow):
        halves = [jnp.split(w, 2, axis=1) for w in narrow]
        low = jnp.concatenate([h[0] for h in halves], axis=1)
        high = jnp.concatenate([h[1] for h in halves], axis=1)
        first = self.core == 0
        mine = jnp.where(first, low, high)
        other = self.swap(jnp.where(first, high, low))
        return jnp.concatenate(self.in_core_order(mine, other), axis=0)

    def tiled(self, blocks):
        tiles = [b.reshape(b.shape[0], -1, LANES).transpose(1, 0, 2).reshape(-1, LANES) for b in blocks]
        return jnp.concatenate(tiles, axis=0)

    def gather_near(self, block):
        got = block[None]
        for digit in reversed(range(self.digits)):
            got = jnp.concatenate(
                [got] + [self.swap(got, j << (2 * digit + 1)) for j in (1, 2, 3)], axis=0
            )
        return got

    def shares(self, parts, digit):
        here = (self.chip >> (2 * digit)) % 4
        out = []
        for j in range(4):
            total = None
            for part in parts:
                cut = part.reshape(part.shape[0] // 4, 4, -1, LANES)
                value = lax.dynamic_index_in_dim(cut, here ^ j, 1, keepdims=False).astype(F32)
                total = value if total is None else total + value
            out.append(total if j == 0 else total.astype(BF))
        return out

    def trade(self, shares, digit):
        return [shares[0]] + [self.swap(shares[j], j << (2 * digit + 1)) for j in (1, 2, 3)]

    def total(self, parts):
        value = parts[0]
        for part in parts[1:]:
            value = value + part.astype(F32)
        return value[0]

    def split_narrow(self, total, pack):
        rows = pack.pair // 2
        count = sum(cols // (2 * LANES) for _, cols in pack.narrow)
        tiles = total[: count * pack.pair].reshape(-1, 2, rows, LANES)
        mine = lax.dynamic_index_in_dim(tiles, self.core, 1, keepdims=False)
        other = self.swap(lax.dynamic_index_in_dim(tiles, 1 - self.core, 1, keepdims=False))
        halves = self.in_core_order(mine, other)
        outs, at = [], 0
        for _, cols in pack.narrow:
            t = cols // (2 * LANES)
            both = jnp.stack([h[at : at + t] for h in halves])
            outs.append(both.transpose(2, 0, 1, 3).reshape(rows, cols))
            at += t
        return outs

    def split_tall(self, total, pack):
        outs = []
        for (rows, cols), at in zip(pack.tall, pack.tall_at):
            own, t = rows // self.n, cols // LANES
            piece = total[at : at + t * own].reshape(t, own, LANES)
            outs.append(piece.transpose(1, 0, 2).reshape(own, cols))
        return outs


def on_device(
    device_count,
    tokens,
    cotangent,
    seq_lens,
    seq_starts,
    input_gain,
    w_query,
    w_key,
    w_value,
    query_gain,
    key_gain,
    w_output,
    attn_post_gain,
    ffn_pre_gain,
    w_gate,
    w_up,
    w_down,
    ffn_post_gain,
):
    mover = Mover(device_count)
    chips = mover.chips
    slots, model = tokens.shape
    hd = w_key.shape[1]
    heads = w_query.shape[1] // hd
    ffn = Pack(
        chips,
        [(model, w_gate.shape[1]), (model, w_up.shape[1])],
        [(w_output.shape[0] * device_count, model), (w_down.shape[0] * device_count, model)],
    )
    attn = Pack(chips, [(model, heads * hd), (model, hd), (model, hd)], [])

    gains = [input_gain, query_gain, key_gain, attn_post_gain, ffn_pre_gain, ffn_post_gain]
    flat = jnp.concatenate(gains)
    flat = jnp.pad(flat, (0, 8 * LANES - flat.shape[0])).reshape(8, LANES)
    narrow = mover.trade_halves([w_gate, w_up, w_query, w_key, w_value])
    split = w_gate.shape[1]
    far = lax.all_gather(mover.tiled([narrow[:, :split], w_output, w_down]), AX, axis=0)
    gathered = far.reshape(chips, 2, ffn.used, LANES)
    mine = mover.gather_near(mover.tiled([narrow[:, split:], flat]))
    other = mover.swap(mine)
    both = jnp.stack(mover.in_core_order(mine[:, attn.used], other[:, attn.used]), axis=1)
    order = [int("".join(reversed(format_base4(k, mover.digits))), 4) for k in range(chips)]
    wanted = jnp.arange(chips, dtype=jnp.int32)[:, None] == (jnp.array(order, jnp.int32) ^ mover.chip)[None]
    flat = mm(wanted.astype(BF), both.reshape(chips, 2 * LANES)).reshape(device_count, LANES)
    vectors, at = [], 0
    for g in gains:
        vectors.append(flat[:, at : at + g.shape[0]].reshape(1, -1))
        at += g.shape[0]
    gin, gq, gk, gpost, gpre, gffn = vectors

    slot = jnp.arange(slots, dtype=jnp.int32)
    inside = (slot[None, :] >= seq_starts[:, None]) & (
        slot[None, :] < seq_starts[:, None] + seq_lens[:, None]
    )
    offset = jnp.sum(jnp.where(inside, seq_starts[:, None], 0), axis=0)
    frequency = rope_base ** (-2.0 * jnp.arange(hd // 2, dtype=F32) / hd)
    angles = (slot - offset).astype(F32)[:, None] * frequency[None, :]
    cos, sin = jnp.cos(angles), jnp.sin(angles)
    core = mover.core.astype(jnp.int32).reshape(1)

    place = jnp.stack([mover.core, mover.chip]).astype(jnp.int32)
    weights, h1, qraw, kraw, qn, kn, v, ob = run_forward(
        attn, heads, seq_lens, seq_starts, place, mine, other, tokens, cos, sin, gin, gq, gk
    )
    result, dx1, dob, dgains, keep, send = run_middle(
        ffn, seq_lens, seq_starts, core, gathered, tokens, ob, cotangent, gpost, gpre, gffn
    )
    shares = mover.shares([keep, mover.swap(send)], 0)
    dob, shares = lax.optimization_barrier((dob, shares))
    ffn_parts = mover.trade(shares, 0)
    grad_tokens, dgin, dgq, dgk, keep, send = run_backward(
        attn, heads, seq_lens, seq_starts, core, weights, tokens, dx1, h1, qraw, kraw, qn, dob, kn, v,
        cos, sin, gin, gq, gk,
    )
    dffn, dpre, dpost = (jnp.sum(dgains[i], axis=0) for i in range(3))
    grads = [jnp.sum(dgin, axis=0), jnp.sum(dgq, axis=0), jnp.sum(dgk, axis=0), dpost, dpre, dffn]
    flat = jnp.concatenate([g.reshape(device_count, -1) for g in grads], axis=1).astype(BF)
    flat = jnp.pad(flat, ((0, 0), (0, 8 * LANES - flat.shape[1]))).reshape(chips, 2, 8, LANES)
    keep = jnp.concatenate(
        [keep, lax.dynamic_index_in_dim(flat, mover.core, 1, keepdims=False)], axis=1
    )
    send = jnp.concatenate(
        [send, lax.dynamic_index_in_dim(flat, 1 - mover.core, 1, keepdims=False)], axis=1
    )
    send, ffn_parts = lax.optimization_barrier((send, ffn_parts))
    attn_parts = [keep, mover.swap(send)]
    for d in range(mover.digits):
        if d > 0:
            ffn_parts = mover.trade(mover.shares(ffn_parts, d), d)
        attn_parts = mover.trade(mover.shares(attn_parts, d), d)
    ffn_sum, attn_sum = mover.total(ffn_parts), mover.total(attn_parts)
    own_gate, own_up = mover.split_narrow(ffn_sum, ffn)
    own_output, own_down = mover.split_tall(ffn_sum, ffn)
    own_query, own_key, own_value = mover.split_narrow(attn_sum, attn)
    flat = attn_sum[attn.used :].reshape(-1)
    owned, at = [], 0
    for g in gains:
        owned.append(flat[at : at + g.shape[0]])
        at += g.shape[0]
    own_gin, own_gq, own_gk, own_gpost, own_gpre, own_gffn = owned
    return (
        result, grad_tokens, own_gin, own_query, own_key, own_value, own_gq, own_gk, own_output, own_gpost,
        own_gpre, own_gate, own_up, own_down, own_gffn,
    )


def solution(mesh):
    rows, flat = P(AX, None), P(AX)
    device_count = mesh.shape[AX]

    def block(*arrays):
        return on_device(device_count, *arrays)

    return jax.shard_map(
        block,
        mesh=mesh,
        in_specs=(
            rows, rows, flat, flat, flat, rows, rows, rows, flat, flat, rows, flat, flat, rows, rows, rows, flat,
        ),
        out_specs=(
            rows, rows, flat, rows, rows, rows, flat, flat, rows, flat, flat, rows, rows, rows, flat,
        ),
        check_vma=False,
    )
```

```python
import functools

import jax
import jax.numpy as jnp
from jax import lax
from jax.experimental import pallas as pl
from jax.experimental.pallas import tpu as pltpu
from jax.sharding import PartitionSpec as P

AX = "fsdp"
epsilon = 1e-06
rope_base = 1000000.0
BF = jnp.bfloat16
F32 = jnp.float32
LANES = 128
TILE = 256
STEP_ROWS = 80
GELU_C = 0.7978845608028654
GELU_K = 0.044715
BIG = -1e30


def mm(a, b):
    return lax.dot_general(a, b, (((1,), (0,)), ((), ())), preferred_element_type=F32)


def mm_bt(a, b):
    return lax.dot_general(a, b, (((1,), (1,)), ((), ())), preferred_element_type=F32)


def mm_at(a, b):
    return lax.dot_general(a, b, (((0,), (0,)), ((), ())), preferred_element_type=F32)


def row_mean(v):
    return jnp.mean(v, axis=-1, keepdims=True)


def fold_rows(v):
    return jnp.sum(v.reshape(v.shape[0] // 8, 8, v.shape[1]), axis=0)


def turn(v, cos, sin):
    half = v.shape[1] // 2
    a, b = v[:, :half], v[:, half:]
    return jnp.concatenate([a * cos - b * sin, b * cos + a * sin], axis=1)


def turn_back(v, cos, sin):
    half = v.shape[1] // 2
    a, b = v[:, :half], v[:, half:]
    return jnp.concatenate([a * cos + b * sin, b * cos - a * sin], axis=1)


def norm_back(du, unit, scale):
    return scale * (du - unit * row_mean(du * unit))


def slot_starts(slot, lens_ref, starts_ref):
    first = slot
    inside = jnp.zeros(slot.shape, F32)
    for s in range(lens_ref.shape[0]):
        member = (slot >= starts_ref[s]) & (slot < starts_ref[s] + lens_ref[s])
        first = jnp.where(member, starts_ref[s], first)
        inside = jnp.where(member, 1.0, inside)
    return first, inside


class Pack:
    def __init__(self, chips, narrow, tall):
        self.chips = chips
        self.narrow = narrow
        self.tall = tall
        self.pair = narrow[0][0] // chips
        self.chips_per_step = STEP_ROWS // self.pair
        self.steps = chips // self.chips_per_step
        at = 0
        self.narrow_at = []
        for _, cols in narrow:
            self.narrow_at.append(at)
            at += cols // (2 * LANES) * self.pair
        self.tall_at = []
        for rows, cols in tall:
            self.tall_at.append(at)
            at += cols // LANES * (rows // (2 * chips))
        self.used = at

    def unpack(self, step, slabs, narrow_refs, tall_refs):
        slabs = [[value[: self.used].astype(F32) for value in pair] for pair in slabs]
        at_row = pl.multiple_of(step * STEP_ROWS, 16)
        for (_, cols), start, out in zip(self.narrow, self.narrow_at, narrow_refs):
            tiles = cols // (2 * LANES)
            for p in range(2):
                for t in range(tiles):
                    lo = start + t * self.pair
                    value = jnp.concatenate([s[p][lo : lo + self.pair] for s in slabs], axis=0)
                    col = (p * tiles + t) * LANES
                    out[pl.ds(at_row, STEP_ROWS), col : col + LANES] = value.astype(BF)
        for (rows, cols), start, out in zip(self.tall, self.tall_at, tall_refs):
            own = rows // (2 * self.chips)
            group = self.chips_per_step * 2 * own
            at_tall = pl.multiple_of(step * group, 16)
            for t in range(cols // LANES):
                lo = start + t * own
                value = jnp.concatenate(
                    [s[p][lo : lo + own] for s in slabs for p in range(2)], axis=0
                )
                out[pl.ds(at_tall, group), t * LANES : (t + 1) * LANES] = value.astype(BF)

    def pack(self, step, core, narrow_refs, tall_refs, keep_ref, send_ref):
        at_row = pl.multiple_of(step * STEP_ROWS, 8)
        pieces = [[[] for _ in range(2)] for _ in range(self.chips_per_step)]
        for (_, cols), acc in zip(self.narrow, narrow_refs):
            tiles = cols // (2 * LANES)
            for p in range(2):
                for t in range(tiles):
                    col = (p * tiles + t) * LANES
                    value = acc[pl.ds(at_row, STEP_ROWS), col : col + LANES]
                    for j in range(self.chips_per_step):
                        pieces[j][p].append(value[j * self.pair : (j + 1) * self.pair])
        for (rows, cols), acc in zip(self.tall, tall_refs):
            own = rows // (2 * self.chips)
            group = self.chips_per_step * 2 * own
            at_tall = pl.multiple_of(step * group, 8)
            for t in range(cols // LANES):
                value = acc[pl.ds(at_tall, group), t * LANES : (t + 1) * LANES]
                for j in range(self.chips_per_step):
                    for p in range(2):
                        lo = (2 * j + p) * own
                        pieces[j][p].append(value[lo : lo + own])
        for j in range(self.chips_per_step):
            first = jnp.concatenate(pieces[j][0], axis=0)
            second = jnp.concatenate(pieces[j][1], axis=0)
            keep_ref[j] = jnp.where(core == 0, first, second).astype(BF)
            send_ref[j] = jnp.where(core == 0, second, first).astype(BF)


def forward_kernel(
    pack, heads,
    lens_ref, starts_ref, place_ref, *refs,
):
    count = pack.chips_per_step
    mine_refs, other_refs, refs = refs[:count], refs[count : 2 * count], refs[2 * count :]
    (
        x_ref, cos_ref, sin_ref, gin_ref, gq_ref, gk_ref,
        w_out, h1_ref, qraw_ref, kraw_ref, qn_ref, kn_ref, v_ref, ob_ref,
        w_s, k_s, v_s, bias_s,
    ) = refs
    step = pl.program_id(0)
    hd = gk_ref.shape[1]
    model = x_ref.shape[1]
    wide = heads * hd

    @pl.when(step < pack.steps)
    def _():
        first = place_ref[0] == 0
        slabs = []
        for mine_ref, other_ref in zip(mine_refs, other_refs):
            mine, other = mine_ref[0].astype(F32), other_ref[0].astype(F32)
            slabs.append([jnp.where(first, mine, other), jnp.where(first, other, mine)])
        pack.unpack(step, slabs, [w_s.at[:, :wide], w_s.at[:, wide : wide + hd], w_s.at[:, wide + hd :]], [])
        w_out[...] = w_s[pl.ds(pl.multiple_of(step * STEP_ROWS, 16), STEP_ROWS), :]

    tile = step - pack.steps

    @pl.when(tile >= 0)
    def _():
        x = x_ref[...].astype(F32)
        scale = lax.rsqrt(row_mean(x * x) + epsilon)
        h1 = (x * scale * gin_ref[...]).astype(BF)
        h1_ref[...] = h1
        cos, sin = cos_ref[...], sin_ref[...]
        raw = mm(h1, w_s[:, :wide])
        qraw_ref[...] = raw
        for h in range(heads):
            part = raw[:, h * hd : (h + 1) * hd]
            unit = part * lax.rsqrt(row_mean(part * part) + epsilon)
            qn_ref[:, h * hd : (h + 1) * hd] = (turn(unit * gq_ref[...], cos, sin) * 0.0625).astype(BF)
        kraw = mm(h1, w_s[:, wide : wide + hd])
        kraw_ref[...] = kraw
        unit = kraw * lax.rsqrt(row_mean(kraw * kraw) + epsilon)
        kn = turn(unit * gk_ref[...], cos, sin).astype(BF)
        kn_ref[...] = kn
        v = mm(h1, w_s[:, wide + hd :]).astype(BF)
        v_ref[...] = v
        at = pl.multiple_of(tile * TILE, TILE)
        k_s[pl.ds(at, TILE), :] = kn
        v_s[pl.ds(at, TILE), :] = v

    for c in range(k_s.shape[0] // TILE):

        @pl.when(tile == c)
        def _():
            span = (c + 1) * TILE
            slot = c * TILE + lax.broadcasted_iota(jnp.int32, (TILE, 1), 0)
            first, _ = slot_starts(slot, lens_ref, starts_ref)
            other = lax.broadcasted_iota(jnp.int32, (TILE, span), 1)
            bias_s[:, :span] = jnp.where((other >= first) & (other <= slot), 0.0, BIG)
            for h in range(heads):
                q = qn_ref[:, h * hd : (h + 1) * hd]
                s = mm_bt(q, k_s[:span, :]) + bias_s[:, :span]
                e = jnp.exp(s - jnp.max(s, axis=-1, keepdims=True))
                inv = 1.0 / jnp.sum(e, axis=-1, keepdims=True)
                o = mm((e * inv).astype(BF), v_s[:span, :])
                ob_ref[:, h * hd : (h + 1) * hd] = o.astype(BF)


def middle_kernel(
    pack, tiles,
    lens_ref, starts_ref, core_ref, g_ref, x_ref, ob_ref, ct_ref, gpost_ref, gpre_ref, gffn_ref,
    res_ref, dx1_ref, dob_ref, dgains_ref, keep_ref, send_ref,
    wg_s, wu_s, wo_s, wd_s, ag_s, au_s, ao_s, ad_s, gain_s,
):
    step = pl.program_id(0)

    @pl.when(step == 0)
    def _():
        for ref in (ag_s, au_s, ao_s, ad_s, gain_s):
            ref[...] = jnp.zeros(ref.shape, F32)

    @pl.when(step < pack.steps)
    def _():
        slabs = [[g_ref[j, p] for p in range(2)] for j in range(pack.chips_per_step)]
        pack.unpack(step, slabs, [wg_s, wu_s], [wo_s, wd_s])

    tile = step - pack.steps

    @pl.when((tile >= 0) & (tile < tiles))
    def _():
        slot = tile * TILE + lax.broadcasted_iota(jnp.int32, (TILE, 1), 0)
        _, live = slot_starts(slot, lens_ref, starts_ref)
        ob = ob_ref[...]
        attn = mm(ob, wo_s[...])
        r1 = lax.rsqrt(row_mean(attn * attn) + epsilon)
        na = attn * r1
        x1 = x_ref[...].astype(F32) + na * gpost_ref[...]
        r2 = lax.rsqrt(row_mean(x1 * x1) + epsilon)
        n1 = x1 * r2
        h2 = (n1 * gpre_ref[...]).astype(BF)
        gate = mm(h2, wg_s[...])
        up = mm(h2, wu_s[...])
        th = jnp.tanh(GELU_C * (gate + GELU_K * gate * gate * gate))
        half = 0.5 * (1.0 + th)
        gl = gate * half
        slope = half + 0.5 * gate * (1.0 - th * th) * (GELU_C * (1.0 + 3.0 * GELU_K * gate * gate))
        act = (gl * up).astype(BF)
        f = mm(act, wd_s[...])
        r3 = lax.rsqrt(row_mean(f * f) + epsilon)
        nf = f * r3
        res_ref[...] = (live * (x1 + nf * gffn_ref[...])).astype(BF)
        dy = live * ct_ref[...].astype(F32)
        gain_s[0] += fold_rows(dy * nf)
        df = norm_back(dy * gffn_ref[...], nf, r3).astype(BF)
        dact = mm_bt(df, wd_s[...])
        ad_s[...] += mm_at(act, df)
        dgate = (dact * up * slope).astype(BF)
        dup = (dact * gl).astype(BF)
        ag_s[...] += mm_at(h2, dgate)
        au_s[...] += mm_at(h2, dup)
        dh2 = mm_bt(dgate, wg_s[...]) + mm_bt(dup, wu_s[...])
        gain_s[1] += fold_rows(dh2 * n1)
        dx1 = dy + norm_back(dh2 * gpre_ref[...], n1, r2)
        dx1_ref[...] = dx1
        gain_s[2] += fold_rows(dx1 * na)
        dattn = norm_back(dx1 * gpost_ref[...], na, r1).astype(BF)
        ao_s[...] += mm_at(ob, dattn)
        dob_ref[...] = mm_bt(dattn, wo_s[...]).astype(BF)

    @pl.when(tile >= tiles)
    def _():
        pack.pack(tile - tiles, core_ref[0], [ag_s, au_s], [ao_s, ad_s], keep_ref, send_ref)
        dgains_ref[...] = gain_s[...]


def backward_kernel(
    pack, heads, tiles,
    lens_ref, starts_ref, core_ref, w_ref, x_ref, dx1_ref, h1_ref, qraw_ref, kraw_ref, qn_ref, dob_ref,
    k_ref, v_ref, cos_ref, sin_ref, gin_ref, gq_ref, gk_ref,
    gt_ref, dgin_ref, dgq_ref, dgk_ref, keep_ref, send_ref,
    dq_s, dk_s, dv_s, bias_s, acc_s, dqr_s,
):
    step = pl.program_id(0)
    hd = gk_ref.shape[1]
    wide = heads * hd

    @pl.when(step == 0)
    def _():
        for ref in (dk_s, dv_s, acc_s, dgin_ref, dgq_ref, dgk_ref):
            ref[...] = jnp.zeros(ref.shape, F32)

    for c in range(tiles):

        @pl.when(step == tiles - 1 - c)
        def _():
            span = (c + 1) * TILE
            slot = c * TILE + lax.broadcasted_iota(jnp.int32, (1, TILE), 1)
            first, _ = slot_starts(slot, lens_ref, starts_ref)
            other = lax.broadcasted_iota(jnp.int32, (span, TILE), 0)
            bias_s[:span, :] = jnp.where((other >= first) & (other <= slot), 0.0, BIG)
            for h in range(heads):
                q = qn_ref[:, h * hd : (h + 1) * hd]
                dob = dob_ref[:, h * hd : (h + 1) * hd]
                s = mm_bt(k_ref[:span, :], q) + bias_s[:span, :]
                e = jnp.exp(s - jnp.max(s, axis=0, keepdims=True))
                p = e * (1.0 / jnp.sum(e, axis=0, keepdims=True))
                dv_s[:span, :] += mm(p.astype(BF), dob)
                dp = mm_bt(v_ref[:span, :], dob)
                ds = (p * (dp - jnp.sum(p * dp, axis=0, keepdims=True))).astype(BF)
                dk_s[:span, :] += mm(ds, q)
                dq_s[:, h * hd : (h + 1) * hd] = mm_at(ds, k_ref[:span, :])

    @pl.when(step < tiles)
    def _():
        at = pl.multiple_of((tiles - 1 - step) * TILE, TILE)
        cos, sin = cos_ref[...], sin_ref[...]
        for h in range(heads):
            d = turn_back(dq_s[:, h * hd : (h + 1) * hd], cos, sin) * 0.0625
            part = qraw_ref[:, h * hd : (h + 1) * hd]
            scale = lax.rsqrt(row_mean(part * part) + epsilon)
            unit = part * scale
            dgq_ref[...] += fold_rows(d * unit)
            dqr_s[:, h * hd : (h + 1) * hd] = norm_back(d * gq_ref[...], unit, scale).astype(BF)
        d = turn_back(dk_s[pl.ds(at, TILE), :], cos, sin)
        part = kraw_ref[...]
        scale = lax.rsqrt(row_mean(part * part) + epsilon)
        unit = part * scale
        dgk_ref[...] += fold_rows(d * unit)
        dqr_s[:, wide : wide + hd] = norm_back(d * gk_ref[...], unit, scale).astype(BF)
        dqr_s[:, wide + hd :] = dv_s[pl.ds(at, TILE), :].astype(BF)
        acc_s[...] += mm_at(h1_ref[...], dqr_s[...])
        dh1 = mm_bt(dqr_s[...], w_ref[...])
        x = x_ref[...].astype(F32)
        scale = lax.rsqrt(row_mean(x * x) + epsilon)
        unit = x * scale
        dgin_ref[...] += fold_rows(dh1 * unit)
        gt_ref[...] = dx1_ref[...] + norm_back(dh1 * gin_ref[...], unit, scale)

    @pl.when(step >= tiles)
    def _():
        accs = [acc_s.at[:, :wide], acc_s.at[:, wide : wide + hd], acc_s.at[:, wide + hd :]]
        pack.pack(step - tiles, core_ref[0], accs, [], keep_ref, send_ref)


def smem():
    return pl.BlockSpec(memory_space=pltpu.SMEM)


def whole(shape):
    zeros = (0,) * len(shape)
    return pl.BlockSpec(shape, lambda s: zeros)


def resident(shape):
    zeros = (0,) * len(shape)
    return pl.BlockSpec(shape, lambda s: zeros, pipeline_mode=pl.Buffered(1))


def params(megabytes):
    return pltpu.CompilerParams(
        dimension_semantics=("arbitrary",), vmem_limit_bytes=megabytes * 1024 * 1024
    )


def shape(dims, kind):
    return jax.ShapeDtypeStruct(dims, kind)


def run_forward(pack, heads, lens, starts, place, mine, other, tokens, cos, sin, gin, gq, gk):
    slots, model = tokens.shape
    hd = gk.shape[1]
    wide = heads * hd
    cols = wide + 2 * hd
    last = pack.steps - 1
    count = pack.chips_per_step

    def tile_spec(width):
        return pl.BlockSpec((TILE, width), lambda s, *_: (jnp.maximum(s - pack.steps, 0), 0))

    def fixed(width):
        return pl.BlockSpec((1, width), lambda s, *_: (0, 0))

    def slab(j):
        def index(s, lens_ref, starts_ref, place_ref):
            far = (jnp.minimum(s, last) * count + j) ^ place_ref[1]
            turned = jnp.int32(0)
            left = pack.chips
            while left > 1:
                turned = turned * 4 + far % 4
                far, left = far // 4, left // 4
            return turned, 0, 0

        return pl.BlockSpec((1, mine.shape[1], LANES), index)

    return pl.pallas_call(
        functools.partial(forward_kernel, pack, heads),
        grid_spec=pltpu.PrefetchScalarGridSpec(
            num_scalar_prefetch=3,
            grid=(pack.steps + slots // TILE,),
            in_specs=[slab(j) for j in range(count)] * 2
            + [tile_spec(model), tile_spec(hd // 2), tile_spec(hd // 2), fixed(model), fixed(hd), fixed(hd)],
            out_specs=[
                pl.BlockSpec((STEP_ROWS, cols), lambda s, *_: (jnp.minimum(s, last), 0)),
                tile_spec(model), tile_spec(wide), tile_spec(hd), tile_spec(wide), tile_spec(hd), tile_spec(hd),
                tile_spec(wide),
            ],
            scratch_shapes=[
                pltpu.VMEM((model, cols), BF), pltpu.VMEM((slots, hd), BF), pltpu.VMEM((slots, hd), BF),
                pltpu.VMEM((TILE, slots), F32),
            ],
        ),
        out_shape=[
            shape((model, cols), BF), shape((slots, model), BF), shape((slots, wide), F32),
            shape((slots, hd), F32), shape((slots, wide), BF), shape((slots, hd), BF), shape((slots, hd), BF),
            shape((slots, wide), BF),
        ],
        compiler_params=params(48),
        cost_estimate=pl.CostEstimate(
            flops=2 * slots * model * cols + 4 * slots * slots * wide // 2,
            bytes_accessed=16 * 1024 * 1024, transcendentals=heads * slots * slots,
        ),
        name="attention_forward",
    )(lens, starts, place, *([mine] * count), *([other] * count), tokens, cos, sin, gin, gq, gk)


def run_middle(pack, lens, starts, core, gathered, tokens, ob, cotangent, gpost, gpre, gffn):
    slots, model = tokens.shape
    wide = ob.shape[1]
    ff = pack.narrow[0][1]
    tiles = slots // TILE
    last = pack.steps - 1

    def tile_spec(width):
        return pl.BlockSpec((TILE, width), lambda s: (jnp.clip(s - pack.steps, 0, tiles - 1), 0))

    def out_packed():
        return pl.BlockSpec(
            (pack.chips_per_step, pack.used, LANES),
            lambda s: (jnp.maximum(s - pack.steps - tiles, 0), 0, 0),
        )

    packed = pl.BlockSpec(
        (pack.chips_per_step, 2, gathered.shape[2], LANES), lambda s: (jnp.minimum(s, last), 0, 0, 0)
    )
    return pl.pallas_call(
        functools.partial(middle_kernel, pack, tiles),
        grid=(2 * pack.steps + tiles,),
        in_specs=[
            smem(), smem(), smem(), packed, tile_spec(model), tile_spec(wide), tile_spec(model),
            whole((1, model)), whole((1, model)), whole((1, model)),
        ],
        out_specs=[
            tile_spec(model), tile_spec(model), tile_spec(wide), whole((3, 8, model)), out_packed(), out_packed(),
        ],
        out_shape=[
            shape((slots, model), BF), shape((slots, model), F32), shape((slots, wide), BF),
            shape((3, 8, model), F32),
            shape((pack.chips, pack.used, LANES), BF), shape((pack.chips, pack.used, LANES), BF),
        ],
        scratch_shapes=[
            pltpu.VMEM((model, ff), BF), pltpu.VMEM((model, ff), BF), pltpu.VMEM((wide, model), BF),
            pltpu.VMEM((ff, model), BF),
            pltpu.VMEM((model, ff), F32), pltpu.VMEM((model, ff), F32), pltpu.VMEM((wide, model), F32),
            pltpu.VMEM((ff, model), F32), pltpu.VMEM((3, 8, model), F32),
        ],
        compiler_params=params(60),
        cost_estimate=pl.CostEstimate(
            flops=6 * slots * model * (3 * ff + wide), bytes_accessed=36 * 1024 * 1024,
            transcendentals=slots * ff,
        ),
        name="output_and_ffn",
    )(lens, starts, core, gathered, tokens, ob, cotangent, gpost, gpre, gffn)


def run_backward(pack, heads, lens, starts, core, weights, tokens, dx1, h1, qraw, kraw, qn, dob, kn, v, cos, sin, gin, gq, gk):
    slots, model = tokens.shape
    hd = gk.shape[1]
    wide = heads * hd
    cols = wide + 2 * hd
    tiles = slots // TILE

    def tile_spec(width):
        return pl.BlockSpec((TILE, width), lambda s: (jnp.maximum(tiles - 1 - s, 0), 0))

    def out_packed():
        return pl.BlockSpec(
            (pack.chips_per_step, pack.used, LANES), lambda s: (jnp.maximum(s - tiles, 0), 0, 0)
        )

    return pl.pallas_call(
        functools.partial(backward_kernel, pack, heads, tiles),
        grid=(tiles + pack.steps,),
        in_specs=[
            smem(), smem(), smem(), resident((model, cols)), tile_spec(model), tile_spec(model), tile_spec(model),
            tile_spec(wide), tile_spec(hd), tile_spec(wide), tile_spec(wide), resident((slots, hd)), resident((slots, hd)),
            tile_spec(hd // 2), tile_spec(hd // 2), whole((1, model)), whole((1, hd)), whole((1, hd)),
        ],
        out_specs=[
            tile_spec(model), whole((8, model)), whole((8, hd)), whole((8, hd)), out_packed(), out_packed(),
        ],
        out_shape=[
            shape((slots, model), F32), shape((8, model), F32), shape((8, hd), F32), shape((8, hd), F32),
            shape((pack.chips, pack.used, LANES), BF), shape((pack.chips, pack.used, LANES), BF),
        ],
        scratch_shapes=[
            pltpu.VMEM((TILE, wide), F32), pltpu.VMEM((slots, hd), F32), pltpu.VMEM((slots, hd), F32),
            pltpu.VMEM((slots, TILE), F32), pltpu.VMEM((model, cols), F32), pltpu.VMEM((TILE, cols), BF),
        ],
        compiler_params=params(56),
        cost_estimate=pl.CostEstimate(
            flops=4 * slots * model * cols + 10 * slots * slots * wide // 2,
            bytes_accessed=24 * 1024 * 1024, transcendentals=heads * slots * slots,
        ),
        name="attention_backward",
    )(lens, starts, core, weights, tokens, dx1, h1, qraw, kraw, qn, dob, kn, v, cos, sin, gin, gq, gk)


def format_base4(value, digits):
    return [str((value >> (2 * d)) % 4) for d in reversed(range(digits))]


class Mover:
    def __init__(self, device_count):
        self.n = device_count
        self.chips = device_count // 2
        self.digits = 0
        while 4 ** (self.digits + 1) <= self.chips:
            self.digits += 1
        me = lax.axis_index(AX)
        self.core = me % 2
        self.chip = me // 2

    def swap(self, value, mask=1):
        return lax.ppermute(value, AX, [(i, i ^ mask) for i in range(self.n)])

    def in_core_order(self, mine, other):
        first = self.core == 0
        return jnp.where(first, mine, other), jnp.where(first, other, mine)

    def trade_halves(self, narrow):
        halves = [jnp.split(w, 2, axis=1) for w in narrow]
        low = jnp.concatenate([h[0] for h in halves], axis=1)
        high = jnp.concatenate([h[1] for h in halves], axis=1)
        first = self.core == 0
        mine = jnp.where(first, low, high)
        other = self.swap(jnp.where(first, high, low))
        return jnp.concatenate(self.in_core_order(mine, other), axis=0)

    def tiled(self, blocks):
        tiles = [b.reshape(b.shape[0], -1, LANES).transpose(1, 0, 2).reshape(-1, LANES) for b in blocks]
        return jnp.concatenate(tiles, axis=0)

    def gather_near(self, block):
        got = block[None]
        for digit in reversed(range(self.digits)):
            got = jnp.concatenate(
                [got] + [self.swap(got, j << (2 * digit + 1)) for j in (1, 2, 3)], axis=0
            )
        return got

    def by_digits(self, value):
        return value.reshape((4,) * self.digits + value.shape[1:])

    def shares(self, parts, digit, left):
        here = (self.chip >> (2 * digit)) % 4
        axis = left.index(digit)
        out = []
        for j in range(4):
            total = None
            for part in parts:
                value = lax.dynamic_index_in_dim(part, here ^ j, axis, keepdims=False).astype(F32)
                total = value if total is None else total + value
            out.append(total if j == 0 else total.astype(BF))
        return out

    def scatter(self, value, digit):
        step = 2 * 4**digit
        firsts = [i for i in range(self.n) if i // step % 4 == 0]
        groups = [[i + k * step for k in range(4)] for i in firsts]
        return lax.psum_scatter(value, AX, scatter_dimension=0, axis_index_groups=groups)

    def trade(self, shares, digit):
        return [shares[0]] + [self.swap(shares[j], j << (2 * digit + 1)) for j in (1, 2, 3)]

    def total(self, parts):
        value = parts[0].astype(F32)
        for part in parts[1:]:
            value = value + part.astype(F32)
        return value

    def split_narrow(self, total, pack):
        rows = pack.pair // 2
        count = sum(cols // (2 * LANES) for _, cols in pack.narrow)
        tiles = total[: count * pack.pair].reshape(-1, 2, rows, LANES)
        mine = lax.dynamic_index_in_dim(tiles, self.core, 1, keepdims=False)
        other = self.swap(lax.dynamic_index_in_dim(tiles, 1 - self.core, 1, keepdims=False))
        halves = self.in_core_order(mine, other)
        outs, at = [], 0
        for _, cols in pack.narrow:
            t = cols // (2 * LANES)
            both = jnp.stack([h[at : at + t] for h in halves])
            outs.append(both.transpose(2, 0, 1, 3).reshape(rows, cols))
            at += t
        return outs

    def split_tall(self, total, pack):
        outs = []
        for (rows, cols), at in zip(pack.tall, pack.tall_at):
            own, t = rows // self.n, cols // LANES
            piece = total[at : at + t * own].reshape(t, own, LANES)
            outs.append(piece.transpose(1, 0, 2).reshape(own, cols))
        return outs


def on_device(
    device_count,
    tokens,
    cotangent,
    seq_lens,
    seq_starts,
    input_gain,
    w_query,
    w_key,
    w_value,
    query_gain,
    key_gain,
    w_output,
    attn_post_gain,
    ffn_pre_gain,
    w_gate,
    w_up,
    w_down,
    ffn_post_gain,
):
    mover = Mover(device_count)
    chips = mover.chips
    slots, model = tokens.shape
    hd = w_key.shape[1]
    heads = w_query.shape[1] // hd
    ffn = Pack(
        chips,
        [(model, w_gate.shape[1]), (model, w_up.shape[1])],
        [(w_output.shape[0] * device_count, model), (w_down.shape[0] * device_count, model)],
    )
    attn = Pack(chips, [(model, heads * hd), (model, hd), (model, hd)], [])

    gains = [input_gain, query_gain, key_gain, attn_post_gain, ffn_pre_gain, ffn_post_gain]
    flat = jnp.concatenate(gains)
    flat = jnp.pad(flat, (0, 8 * LANES - flat.shape[0])).reshape(8, LANES)
    narrow = mover.trade_halves([w_gate, w_up, w_query, w_key, w_value])
    split = w_gate.shape[1]
    far = lax.all_gather(mover.tiled([narrow[:, :split], w_output, w_down]), AX, axis=0)
    gathered = far.reshape(chips, 2, ffn.used, LANES)
    mine = mover.gather_near(mover.tiled([narrow[:, split:], flat]))
    other = mover.swap(mine)
    both = jnp.stack(mover.in_core_order(mine[:, attn.used], other[:, attn.used]), axis=1)
    order = [int("".join(reversed(format_base4(k, mover.digits))), 4) for k in range(chips)]
    wanted = jnp.arange(chips, dtype=jnp.int32)[:, None] == (jnp.array(order, jnp.int32) ^ mover.chip)[None]
    flat = mm(wanted.astype(BF), both.reshape(chips, 2 * LANES)).reshape(device_count, LANES)
    vectors, at = [], 0
    for g in gains:
        vectors.append(flat[:, at : at + g.shape[0]].reshape(1, -1))
        at += g.shape[0]
    gin, gq, gk, gpost, gpre, gffn = vectors

    slot = jnp.arange(slots, dtype=jnp.int32)
    inside = (slot[None, :] >= seq_starts[:, None]) & (
        slot[None, :] < seq_starts[:, None] + seq_lens[:, None]
    )
    offset = jnp.sum(jnp.where(inside, seq_starts[:, None], 0), axis=0)
    frequency = rope_base ** (-2.0 * jnp.arange(hd // 2, dtype=F32) / hd)
    angles = (slot - offset).astype(F32)[:, None] * frequency[None, :]
    cos, sin = jnp.cos(angles), jnp.sin(angles)
    core = mover.core.astype(jnp.int32).reshape(1)

    place = jnp.stack([mover.core, mover.chip]).astype(jnp.int32)
    weights, h1, qraw, kraw, qn, kn, v, ob = run_forward(
        attn, heads, seq_lens, seq_starts, place, mine, other, tokens, cos, sin, gin, gq, gk
    )
    result, dx1, dob, dgains, keep, send = run_middle(
        ffn, seq_lens, seq_starts, core, gathered, tokens, ob, cotangent, gpost, gpre, gffn
    )
    up, down = list(range(mover.digits)), list(reversed(range(mover.digits)))
    cut = 3 * ffn.used // 32 * 8
    both = [mover.by_digits(keep), mover.by_digits(mover.swap(send))]
    near = mover.shares([v[..., :cut, :] for v in both], up[0], down)
    far = mover.total([v[..., cut:, :] for v in both]).astype(BF)
    dob, near, far = lax.optimization_barrier((dob, near, far))
    near = mover.trade(near, up[0])
    far = mover.scatter(far, down[0])
    grad_tokens, dgin, dgq, dgk, keep, send = run_backward(
        attn, heads, seq_lens, seq_starts, core, weights, tokens, dx1, h1, qraw, kraw, qn, dob, kn, v,
        cos, sin, gin, gq, gk,
    )
    dffn, dpre, dpost = (jnp.sum(dgains[i], axis=0) for i in range(3))
    grads = [jnp.sum(dgin, axis=0), jnp.sum(dgq, axis=0), jnp.sum(dgk, axis=0), dpost, dpre, dffn]
    flat = jnp.concatenate([g.reshape(device_count, -1) for g in grads], axis=1).astype(BF)
    flat = jnp.pad(flat, ((0, 0), (0, 8 * LANES - flat.shape[1]))).reshape(chips, 2, 8, LANES)
    keep = jnp.concatenate(
        [keep, lax.dynamic_index_in_dim(flat, mover.core, 1, keepdims=False)], axis=1
    )
    send = jnp.concatenate(
        [send, lax.dynamic_index_in_dim(flat, 1 - mover.core, 1, keepdims=False)], axis=1
    )
    send, near, far = lax.optimization_barrier((send, near, far))
    attn_parts = [mover.by_digits(keep), mover.by_digits(mover.swap(send))]
    for d in down[1:]:
        far = mover.scatter(far, d)
    for d in up:
        share = mover.shares(attn_parts, d, [k for k in down if k >= d])
        if d + 1 < mover.digits:
            near = mover.shares(near, d + 1, [k for k in down if k > d])
            share, near = lax.optimization_barrier((share, near))
            near = mover.trade(near, d + 1)
        attn_parts = mover.trade(share, d)
    far, attn_parts = lax.optimization_barrier((far, attn_parts))
    ffn_sum = jnp.concatenate([mover.total(near), far.astype(F32)], axis=0)
    attn_sum = mover.total(attn_parts)
    own_gate, own_up = mover.split_narrow(ffn_sum, ffn)
    own_output, own_down = mover.split_tall(ffn_sum, ffn)
    own_query, own_key, own_value = mover.split_narrow(attn_sum, attn)
    flat = attn_sum[attn.used :].reshape(-1)
    owned, at = [], 0
    for g in gains:
        owned.append(flat[at : at + g.shape[0]])
        at += g.shape[0]
    own_gin, own_gq, own_gk, own_gpost, own_gpre, own_gffn = owned
    return (
        result, grad_tokens, own_gin, own_query, own_key, own_value, own_gq, own_gk, own_output, own_gpost,
        own_gpre, own_gate, own_up, own_down, own_gffn,
    )


def solution(mesh):
    rows, flat = P(AX, None), P(AX)
    device_count = mesh.shape[AX]

    def block(*arrays):
        return on_device(device_count, *arrays)

    return jax.shard_map(
        block,
        mesh=mesh,
        in_specs=(
            rows, rows, flat, flat, flat, rows, rows, rows, flat, flat, rows, flat, flat, rows, rows, rows, flat,
        ),
        out_specs=(
            rows, rows, flat, rows, rows, rows, flat, flat, rows, flat, flat, rows, rows, rows, flat,
        ),
        check_vma=False,
    )
```

```python
import functools

import jax
import jax.numpy as jnp
from jax import lax
from jax.experimental import pallas as pl
from jax.experimental.pallas import tpu as pltpu
from jax.sharding import PartitionSpec as P

AX = "fsdp"
epsilon = 1e-06
rope_base = 1000000.0
BF = jnp.bfloat16
F32 = jnp.float32
LANES = 128
TILE = 256
STEP_ROWS = 80
GELU_C = 0.7978845608028654
GELU_K = 0.044715
BIG = -1e30


def mm(a, b):
    return lax.dot_general(a, b, (((1,), (0,)), ((), ())), preferred_element_type=F32)


def mm_bt(a, b):
    return lax.dot_general(a, b, (((1,), (1,)), ((), ())), preferred_element_type=F32)


def mm_at(a, b):
    return lax.dot_general(a, b, (((0,), (0,)), ((), ())), preferred_element_type=F32)


def row_mean(v):
    return jnp.mean(v, axis=-1, keepdims=True)


def fold_rows(v):
    return jnp.sum(v.reshape(v.shape[0] // 8, 8, v.shape[1]), axis=0)


def turn(v, cos, sin):
    half = v.shape[1] // 2
    a, b = v[:, :half], v[:, half:]
    return jnp.concatenate([a * cos - b * sin, b * cos + a * sin], axis=1)


def turn_back(v, cos, sin):
    half = v.shape[1] // 2
    a, b = v[:, :half], v[:, half:]
    return jnp.concatenate([a * cos + b * sin, b * cos - a * sin], axis=1)


def norm_back(du, unit, scale):
    return scale * (du - unit * row_mean(du * unit))


def slot_starts(slot, lens_ref, starts_ref):
    first = slot
    inside = jnp.zeros(slot.shape, F32)
    for s in range(lens_ref.shape[0]):
        member = (slot >= starts_ref[s]) & (slot < starts_ref[s] + lens_ref[s])
        first = jnp.where(member, starts_ref[s], first)
        inside = jnp.where(member, 1.0, inside)
    return first, inside


class Pack:
    def __init__(self, chips, narrow, tall):
        self.chips = chips
        self.narrow = narrow
        self.tall = tall
        self.pair = narrow[0][0] // chips
        self.chips_per_step = STEP_ROWS // self.pair
        self.steps = chips // self.chips_per_step
        at = 0
        self.narrow_at = []
        for _, cols in narrow:
            self.narrow_at.append(at)
            at += cols // (2 * LANES) * self.pair
        self.wide_rows = at
        self.tall_at = []
        for rows, cols in tall:
            self.tall_at.append(at)
            at += cols // LANES * (rows // (2 * chips))
        self.used = at

    def unpack(self, step, slabs, narrow_refs, tall_slabs, tall_refs):
        slabs = [[value[: self.wide_rows].astype(F32) for value in pair] for pair in slabs]
        at_row = pl.multiple_of(step * STEP_ROWS, 16)
        for (_, cols), start, out in zip(self.narrow, self.narrow_at, narrow_refs):
            tiles = cols // (2 * LANES)
            for p in range(2):
                for t in range(tiles):
                    lo = start + t * self.pair
                    value = jnp.concatenate([s[p][lo : lo + self.pair] for s in slabs], axis=0)
                    col = (p * tiles + t) * LANES
                    out[pl.ds(at_row, STEP_ROWS), col : col + LANES] = value.astype(BF)
        for (rows, cols), start, out in zip(self.tall, self.tall_at, tall_refs):
            own = rows // (2 * self.chips)
            group = self.chips_per_step * 2 * own
            at_tall = pl.multiple_of(step * group, 16)
            for t in range(cols // LANES):
                lo = start - self.wide_rows + t * own
                value = jnp.concatenate(
                    [s[p][lo : lo + own] for s in tall_slabs for p in range(2)], axis=0
                )
                out[pl.ds(at_tall, group), t * LANES : (t + 1) * LANES] = value.astype(BF)

    def pack(self, step, core, narrow_refs, tall_refs, keep_ref, send_ref):
        at_row = pl.multiple_of(step * STEP_ROWS, 8)
        pieces = [[[] for _ in range(2)] for _ in range(self.chips_per_step)]
        for (_, cols), acc in zip(self.narrow, narrow_refs):
            tiles = cols // (2 * LANES)
            for p in range(2):
                for t in range(tiles):
                    col = (p * tiles + t) * LANES
                    value = acc[pl.ds(at_row, STEP_ROWS), col : col + LANES]
                    for j in range(self.chips_per_step):
                        pieces[j][p].append(value[j * self.pair : (j + 1) * self.pair])
        for (rows, cols), acc in zip(self.tall, tall_refs):
            own = rows // (2 * self.chips)
            group = self.chips_per_step * 2 * own
            at_tall = pl.multiple_of(step * group, 8)
            for t in range(cols // LANES):
                value = acc[pl.ds(at_tall, group), t * LANES : (t + 1) * LANES]
                for j in range(self.chips_per_step):
                    for p in range(2):
                        lo = (2 * j + p) * own
                        pieces[j][p].append(value[lo : lo + own])
        for j in range(self.chips_per_step):
            first = jnp.concatenate(pieces[j][0], axis=0)
            second = jnp.concatenate(pieces[j][1], axis=0)
            keep_ref[j] = jnp.where(core == 0, first, second).astype(BF)
            send_ref[j] = jnp.where(core == 0, second, first).astype(BF)


def near_slabs(place_ref, mine_refs, other_refs):
    first = place_ref[0] == 0
    slabs = []
    for mine_ref, other_ref in zip(mine_refs, other_refs):
        mine, other = mine_ref[0].astype(F32), other_ref[0].astype(F32)
        slabs.append([jnp.where(first, mine, other), jnp.where(first, other, mine)])
    return slabs


def near_specs(pack, rows):
    def slab(j):
        def index(s, lens_ref, starts_ref, place_ref):
            far = (jnp.minimum(s, pack.steps - 1) * pack.chips_per_step + j) ^ place_ref[1]
            turned = jnp.int32(0)
            left = pack.chips
            while left > 1:
                turned = turned * 4 + far % 4
                far, left = far // 4, left // 4
            return turned, 0, 0

        return pl.BlockSpec((1, rows, LANES), index)

    return [slab(j) for j in range(pack.chips_per_step)]


def forward_kernel(
    pack, heads,
    lens_ref, starts_ref, place_ref, *refs,
):
    count = pack.chips_per_step
    mine_refs, other_refs, refs = refs[:count], refs[count : 2 * count], refs[2 * count :]
    (
        x_ref, cos_ref, sin_ref, gin_ref, gq_ref, gk_ref,
        w_out, h1_ref, qraw_ref, kraw_ref, qn_ref, kn_ref, v_ref, ob_ref,
        w_s, k_s, v_s, bias_s,
    ) = refs
    step = pl.program_id(0)
    hd = gk_ref.shape[1]
    model = x_ref.shape[1]
    wide = heads * hd

    @pl.when(step < pack.steps)
    def _():
        slabs = near_slabs(place_ref, mine_refs, other_refs)
        pack.unpack(step, slabs, [w_s.at[:, :wide], w_s.at[:, wide : wide + hd], w_s.at[:, wide + hd :]], [], [])
        w_out[...] = w_s[pl.ds(pl.multiple_of(step * STEP_ROWS, 16), STEP_ROWS), :]

    tile = step - pack.steps

    @pl.when(tile >= 0)
    def _():
        x = x_ref[...].astype(F32)
        scale = lax.rsqrt(row_mean(x * x) + epsilon)
        h1 = (x * scale * gin_ref[...]).astype(BF)
        h1_ref[...] = h1
        cos, sin = cos_ref[...], sin_ref[...]
        raw = mm(h1, w_s[:, :wide])
        qraw_ref[...] = raw
        for h in range(heads):
            part = raw[:, h * hd : (h + 1) * hd]
            unit = part * lax.rsqrt(row_mean(part * part) + epsilon)
            qn_ref[:, h * hd : (h + 1) * hd] = (turn(unit * gq_ref[...], cos, sin) * 0.0625).astype(BF)
        kraw = mm(h1, w_s[:, wide : wide + hd])
        kraw_ref[...] = kraw
        unit = kraw * lax.rsqrt(row_mean(kraw * kraw) + epsilon)
        kn = turn(unit * gk_ref[...], cos, sin).astype(BF)
        kn_ref[...] = kn
        v = mm(h1, w_s[:, wide + hd :]).astype(BF)
        v_ref[...] = v
        at = pl.multiple_of(tile * TILE, TILE)
        k_s[pl.ds(at, TILE), :] = kn
        v_s[pl.ds(at, TILE), :] = v

    for c in range(k_s.shape[0] // TILE):

        @pl.when(tile == c)
        def _():
            span = (c + 1) * TILE
            slot = c * TILE + lax.broadcasted_iota(jnp.int32, (TILE, 1), 0)
            first, _ = slot_starts(slot, lens_ref, starts_ref)
            other = lax.broadcasted_iota(jnp.int32, (TILE, span), 1)
            bias_s[:, :span] = jnp.where((other >= first) & (other <= slot), 0.0, BIG)
            for h in range(heads):
                q = qn_ref[:, h * hd : (h + 1) * hd]
                s = mm_bt(q, k_s[:span, :]) + bias_s[:, :span]
                e = jnp.exp(s - jnp.max(s, axis=-1, keepdims=True))
                inv = 1.0 / jnp.sum(e, axis=-1, keepdims=True)
                o = mm((e * inv).astype(BF), v_s[:span, :])
                ob_ref[:, h * hd : (h + 1) * hd] = o.astype(BF)


def middle_kernel(
    pack, tiles,
    lens_ref, starts_ref, place_ref, *refs,
):
    count = pack.chips_per_step
    mine_refs, other_refs, refs = refs[:count], refs[count : 2 * count], refs[2 * count :]
    (
        g_ref, x_ref, ob_ref, ct_ref, gpost_ref, gpre_ref, gffn_ref,
        res_ref, dx1_ref, dob_ref, dgains_ref, keep_ref, send_ref,
        wg_s, wu_s, wo_s, wd_s, ag_s, au_s, ao_s, ad_s, gain_s,
    ) = refs
    step = pl.program_id(0)

    @pl.when(step == 0)
    def _():
        for ref in (ag_s, au_s, ao_s, ad_s, gain_s):
            ref[...] = jnp.zeros(ref.shape, F32)

    @pl.when(step < pack.steps)
    def _():
        slabs = [[g_ref[j, p] for p in range(2)] for j in range(pack.chips_per_step)]
        pack.unpack(step, slabs, [wg_s, wu_s], near_slabs(place_ref, mine_refs, other_refs), [wo_s, wd_s])

    tile = step - pack.steps

    @pl.when((tile >= 0) & (tile < tiles))
    def _():
        slot = tile * TILE + lax.broadcasted_iota(jnp.int32, (TILE, 1), 0)
        _, live = slot_starts(slot, lens_ref, starts_ref)
        ob = ob_ref[...]
        attn = mm(ob, wo_s[...])
        r1 = lax.rsqrt(row_mean(attn * attn) + epsilon)
        na = attn * r1
        x1 = x_ref[...].astype(F32) + na * gpost_ref[...]
        r2 = lax.rsqrt(row_mean(x1 * x1) + epsilon)
        n1 = x1 * r2
        h2 = (n1 * gpre_ref[...]).astype(BF)
        gate = mm(h2, wg_s[...])
        up = mm(h2, wu_s[...])
        th = jnp.tanh(GELU_C * (gate + GELU_K * gate * gate * gate))
        half = 0.5 * (1.0 + th)
        gl = gate * half
        slope = half + 0.5 * gate * (1.0 - th * th) * (GELU_C * (1.0 + 3.0 * GELU_K * gate * gate))
        act = (gl * up).astype(BF)
        f = mm(act, wd_s[...])
        r3 = lax.rsqrt(row_mean(f * f) + epsilon)
        nf = f * r3
        res_ref[...] = (live * (x1 + nf * gffn_ref[...])).astype(BF)
        dy = live * ct_ref[...].astype(F32)
        gain_s[0] += fold_rows(dy * nf)
        df = norm_back(dy * gffn_ref[...], nf, r3).astype(BF)
        dact = mm_bt(df, wd_s[...])
        ad_s[...] += mm_at(act, df)
        dgate = (dact * up * slope).astype(BF)
        dup = (dact * gl).astype(BF)
        ag_s[...] += mm_at(h2, dgate)
        au_s[...] += mm_at(h2, dup)
        dh2 = mm_bt(dgate, wg_s[...]) + mm_bt(dup, wu_s[...])
        gain_s[1] += fold_rows(dh2 * n1)
        dx1 = dy + norm_back(dh2 * gpre_ref[...], n1, r2)
        dx1_ref[...] = dx1
        gain_s[2] += fold_rows(dx1 * na)
        dattn = norm_back(dx1 * gpost_ref[...], na, r1).astype(BF)
        ao_s[...] += mm_at(ob, dattn)
        dob_ref[...] = mm_bt(dattn, wo_s[...]).astype(BF)

    @pl.when(tile >= tiles)
    def _():
        pack.pack(tile - tiles, place_ref[0], [ag_s, au_s], [ao_s, ad_s], keep_ref, send_ref)
        dgains_ref[...] = gain_s[...]


def backward_kernel(
    pack, heads, tiles,
    lens_ref, starts_ref, core_ref, w_ref, x_ref, dx1_ref, h1_ref, qraw_ref, kraw_ref, qn_ref, dob_ref,
    k_ref, v_ref, cos_ref, sin_ref, gin_ref, gq_ref, gk_ref,
    gt_ref, dgin_ref, dgq_ref, dgk_ref, keep_ref, send_ref,
    dq_s, dk_s, dv_s, bias_s, acc_s, dqr_s,
):
    step = pl.program_id(0)
    hd = gk_ref.shape[1]
    wide = heads * hd

    @pl.when(step == 0)
    def _():
        for ref in (dk_s, dv_s, acc_s, dgin_ref, dgq_ref, dgk_ref):
            ref[...] = jnp.zeros(ref.shape, F32)

    for c in range(tiles):

        @pl.when(step == tiles - 1 - c)
        def _():
            span = (c + 1) * TILE
            slot = c * TILE + lax.broadcasted_iota(jnp.int32, (1, TILE), 1)
            first, _ = slot_starts(slot, lens_ref, starts_ref)
            other = lax.broadcasted_iota(jnp.int32, (span, TILE), 0)
            bias_s[:span, :] = jnp.where((other >= first) & (other <= slot), 0.0, BIG)
            for h in range(heads):
                q = qn_ref[:, h * hd : (h + 1) * hd]
                dob = dob_ref[:, h * hd : (h + 1) * hd]
                s = mm_bt(k_ref[:span, :], q) + bias_s[:span, :]
                e = jnp.exp(s - jnp.max(s, axis=0, keepdims=True))
                p = e * (1.0 / jnp.sum(e, axis=0, keepdims=True))
                dv_s[:span, :] += mm(p.astype(BF), dob)
                dp = mm_bt(v_ref[:span, :], dob)
                ds = (p * (dp - jnp.sum(p * dp, axis=0, keepdims=True))).astype(BF)
                dk_s[:span, :] += mm(ds, q)
                dq_s[:, h * hd : (h + 1) * hd] = mm_at(ds, k_ref[:span, :])

    @pl.when(step < tiles)
    def _():
        at = pl.multiple_of((tiles - 1 - step) * TILE, TILE)
        cos, sin = cos_ref[...], sin_ref[...]
        for h in range(heads):
            d = turn_back(dq_s[:, h * hd : (h + 1) * hd], cos, sin) * 0.0625
            part = qraw_ref[:, h * hd : (h + 1) * hd]
            scale = lax.rsqrt(row_mean(part * part) + epsilon)
            unit = part * scale
            dgq_ref[...] += fold_rows(d * unit)
            dqr_s[:, h * hd : (h + 1) * hd] = norm_back(d * gq_ref[...], unit, scale).astype(BF)
        d = turn_back(dk_s[pl.ds(at, TILE), :], cos, sin)
        part = kraw_ref[...]
        scale = lax.rsqrt(row_mean(part * part) + epsilon)
        unit = part * scale
        dgk_ref[...] += fold_rows(d * unit)
        dqr_s[:, wide : wide + hd] = norm_back(d * gk_ref[...], unit, scale).astype(BF)
        dqr_s[:, wide + hd :] = dv_s[pl.ds(at, TILE), :].astype(BF)
        acc_s[...] += mm_at(h1_ref[...], dqr_s[...])
        dh1 = mm_bt(dqr_s[...], w_ref[...])
        x = x_ref[...].astype(F32)
        scale = lax.rsqrt(row_mean(x * x) + epsilon)
        unit = x * scale
        dgin_ref[...] += fold_rows(dh1 * unit)
        gt_ref[...] = dx1_ref[...] + norm_back(dh1 * gin_ref[...], unit, scale)

    @pl.when(step >= tiles)
    def _():
        accs = [acc_s.at[:, :wide], acc_s.at[:, wide : wide + hd], acc_s.at[:, wide + hd :]]
        pack.pack(step - tiles, core_ref[0], accs, [], keep_ref, send_ref)


def smem():
    return pl.BlockSpec(memory_space=pltpu.SMEM)


def whole(shape):
    zeros = (0,) * len(shape)
    return pl.BlockSpec(shape, lambda s: zeros)


def resident(shape):
    zeros = (0,) * len(shape)
    return pl.BlockSpec(shape, lambda s: zeros, pipeline_mode=pl.Buffered(1))


def params(megabytes):
    return pltpu.CompilerParams(
        dimension_semantics=("arbitrary",), vmem_limit_bytes=megabytes * 1024 * 1024
    )


def shape(dims, kind):
    return jax.ShapeDtypeStruct(dims, kind)


def run_forward(pack, heads, lens, starts, place, mine, other, tokens, cos, sin, gin, gq, gk):
    slots, model = tokens.shape
    hd = gk.shape[1]
    wide = heads * hd
    cols = wide + 2 * hd
    last = pack.steps - 1
    count = pack.chips_per_step

    def tile_spec(width):
        return pl.BlockSpec((TILE, width), lambda s, *_: (jnp.maximum(s - pack.steps, 0), 0))

    def fixed(width):
        return pl.BlockSpec((1, width), lambda s, *_: (0, 0))

    return pl.pallas_call(
        functools.partial(forward_kernel, pack, heads),
        grid_spec=pltpu.PrefetchScalarGridSpec(
            num_scalar_prefetch=3,
            grid=(pack.steps + slots // TILE,),
            in_specs=near_specs(pack, mine.shape[1]) * 2
            + [tile_spec(model), tile_spec(hd // 2), tile_spec(hd // 2), fixed(model), fixed(hd), fixed(hd)],
            out_specs=[
                pl.BlockSpec((STEP_ROWS, cols), lambda s, *_: (jnp.minimum(s, last), 0)),
                tile_spec(model), tile_spec(wide), tile_spec(hd), tile_spec(wide), tile_spec(hd), tile_spec(hd),
                tile_spec(wide),
            ],
            scratch_shapes=[
                pltpu.VMEM((model, cols), BF), pltpu.VMEM((slots, hd), BF), pltpu.VMEM((slots, hd), BF),
                pltpu.VMEM((TILE, slots), F32),
            ],
        ),
        out_shape=[
            shape((model, cols), BF), shape((slots, model), BF), shape((slots, wide), F32),
            shape((slots, hd), F32), shape((slots, wide), BF), shape((slots, hd), BF), shape((slots, hd), BF),
            shape((slots, wide), BF),
        ],
        compiler_params=params(48),
        cost_estimate=pl.CostEstimate(
            flops=2 * slots * model * cols + 4 * slots * slots * wide // 2,
            bytes_accessed=16 * 1024 * 1024, transcendentals=heads * slots * slots,
        ),
        name="attention_forward",
    )(lens, starts, place, *([mine] * count), *([other] * count), tokens, cos, sin, gin, gq, gk)


def run_middle(pack, lens, starts, place, mine, other, gathered, tokens, ob, cotangent, gpost, gpre, gffn):
    slots, model = tokens.shape
    wide = ob.shape[1]
    ff = pack.narrow[0][1]
    tiles = slots // TILE
    last = pack.steps - 1

    def tile_spec(width):
        return pl.BlockSpec((TILE, width), lambda s, *_: (jnp.clip(s - pack.steps, 0, tiles - 1), 0))

    def fixed(dims):
        zeros = (0,) * len(dims)
        return pl.BlockSpec(dims, lambda s, *_: zeros)

    def out_packed():
        return pl.BlockSpec(
            (pack.chips_per_step, pack.used, LANES),
            lambda s, *_: (jnp.maximum(s - pack.steps - tiles, 0), 0, 0),
        )

    packed = pl.BlockSpec(
        (pack.chips_per_step, 2, gathered.shape[2], LANES), lambda s, *_: (jnp.minimum(s, last), 0, 0, 0)
    )
    return pl.pallas_call(
        functools.partial(middle_kernel, pack, tiles),
        grid_spec=pltpu.PrefetchScalarGridSpec(
        num_scalar_prefetch=3,
        grid=(2 * pack.steps + tiles,),
        in_specs=near_specs(pack, mine.shape[1]) * 2 + [
            packed, tile_spec(model), tile_spec(wide), tile_spec(model),
            fixed((1, model)), fixed((1, model)), fixed((1, model)),
        ],
        out_specs=[
            tile_spec(model), tile_spec(model), tile_spec(wide), fixed((3, 8, model)), out_packed(), out_packed(),
        ],
        scratch_shapes=[
            pltpu.VMEM((model, ff), BF), pltpu.VMEM((model, ff), BF), pltpu.VMEM((wide, model), BF),
            pltpu.VMEM((ff, model), BF),
            pltpu.VMEM((model, ff), F32), pltpu.VMEM((model, ff), F32), pltpu.VMEM((wide, model), F32),
            pltpu.VMEM((ff, model), F32), pltpu.VMEM((3, 8, model), F32),
        ],
        ),
        out_shape=[
            shape((slots, model), BF), shape((slots, model), F32), shape((slots, wide), BF),
            shape((3, 8, model), F32),
            shape((pack.chips, pack.used, LANES), BF), shape((pack.chips, pack.used, LANES), BF),
        ],
        compiler_params=params(60),
        cost_estimate=pl.CostEstimate(
            flops=6 * slots * model * (3 * ff + wide), bytes_accessed=36 * 1024 * 1024,
            transcendentals=slots * ff,
        ),
        name="output_and_ffn",
    )(lens, starts, place, *([mine] * pack.chips_per_step), *([other] * pack.chips_per_step), gathered, tokens, ob, cotangent, gpost, gpre, gffn)


def run_backward(pack, heads, lens, starts, core, weights, tokens, dx1, h1, qraw, kraw, qn, dob, kn, v, cos, sin, gin, gq, gk):
    slots, model = tokens.shape
    hd = gk.shape[1]
    wide = heads * hd
    cols = wide + 2 * hd
    tiles = slots // TILE

    def tile_spec(width):
        return pl.BlockSpec((TILE, width), lambda s: (jnp.maximum(tiles - 1 - s, 0), 0))

    def out_packed():
        return pl.BlockSpec(
            (pack.chips_per_step, pack.used, LANES), lambda s: (jnp.maximum(s - tiles, 0), 0, 0)
        )

    return pl.pallas_call(
        functools.partial(backward_kernel, pack, heads, tiles),
        grid=(tiles + pack.steps,),
        in_specs=[
            smem(), smem(), smem(), resident((model, cols)), tile_spec(model), tile_spec(model), tile_spec(model),
            tile_spec(wide), tile_spec(hd), tile_spec(wide), tile_spec(wide), resident((slots, hd)), resident((slots, hd)),
            tile_spec(hd // 2), tile_spec(hd // 2), whole((1, model)), whole((1, hd)), whole((1, hd)),
        ],
        out_specs=[
            tile_spec(model), whole((8, model)), whole((8, hd)), whole((8, hd)), out_packed(), out_packed(),
        ],
        out_shape=[
            shape((slots, model), F32), shape((8, model), F32), shape((8, hd), F32), shape((8, hd), F32),
            shape((pack.chips, pack.used, LANES), BF), shape((pack.chips, pack.used, LANES), BF),
        ],
        scratch_shapes=[
            pltpu.VMEM((TILE, wide), F32), pltpu.VMEM((slots, hd), F32), pltpu.VMEM((slots, hd), F32),
            pltpu.VMEM((slots, TILE), F32), pltpu.VMEM((model, cols), F32), pltpu.VMEM((TILE, cols), BF),
        ],
        compiler_params=params(56),
        cost_estimate=pl.CostEstimate(
            flops=4 * slots * model * cols + 10 * slots * slots * wide // 2,
            bytes_accessed=24 * 1024 * 1024, transcendentals=heads * slots * slots,
        ),
        name="attention_backward",
    )(lens, starts, core, weights, tokens, dx1, h1, qraw, kraw, qn, dob, kn, v, cos, sin, gin, gq, gk)


def format_base4(value, digits):
    return [str((value >> (2 * d)) % 4) for d in reversed(range(digits))]


class Mover:
    def __init__(self, device_count):
        self.n = device_count
        self.chips = device_count // 2
        self.digits = 0
        while 4 ** (self.digits + 1) <= self.chips:
            self.digits += 1
        me = lax.axis_index(AX)
        self.core = me % 2
        self.chip = me // 2

    def swap(self, value, mask=1):
        return lax.ppermute(value, AX, [(i, i ^ mask) for i in range(self.n)])

    def in_core_order(self, mine, other):
        first = self.core == 0
        return jnp.where(first, mine, other), jnp.where(first, other, mine)

    def trade_halves(self, narrow):
        halves = [jnp.split(w, 2, axis=1) for w in narrow]
        low = jnp.concatenate([h[0] for h in halves], axis=1)
        high = jnp.concatenate([h[1] for h in halves], axis=1)
        first = self.core == 0
        mine = jnp.where(first, low, high)
        other = self.swap(jnp.where(first, high, low))
        return jnp.concatenate(self.in_core_order(mine, other), axis=0)

    def tiled(self, blocks):
        tiles = [b.reshape(b.shape[0], -1, LANES).transpose(1, 0, 2).reshape(-1, LANES) for b in blocks]
        return jnp.concatenate(tiles, axis=0)

    def spread(self, got, digit):
        return [got] + [self.swap(got, j << (2 * digit + 1)) for j in (1, 2, 3)]

    def by_digits(self, value):
        return value.reshape((4,) * self.digits + value.shape[1:])

    def shares(self, parts, digit, left):
        here = (self.chip >> (2 * digit)) % 4
        axis = left.index(digit)
        out = []
        for j in range(4):
            total = None
            for part in parts:
                value = lax.dynamic_index_in_dim(part, here ^ j, axis, keepdims=False).astype(F32)
                total = value if total is None else total + value
            out.append(total if j == 0 else total.astype(BF))
        return out

    def scatter(self, value, digit):
        step = 2 * 4**digit
        firsts = [i for i in range(self.n) if i // step % 4 == 0]
        groups = [[i + k * step for k in range(4)] for i in firsts]
        return lax.psum_scatter(value, AX, scatter_dimension=0, axis_index_groups=groups)

    def trade(self, shares, digit):
        return [shares[0]] + [self.swap(shares[j], j << (2 * digit + 1)) for j in (1, 2, 3)]

    def total(self, parts):
        value = parts[0].astype(F32)
        for part in parts[1:]:
            value = value + part.astype(F32)
        return value

    def split_narrow(self, total, pack):
        rows = pack.pair // 2
        count = sum(cols // (2 * LANES) for _, cols in pack.narrow)
        tiles = total[: count * pack.pair].reshape(-1, 2, rows, LANES)
        mine = lax.dynamic_index_in_dim(tiles, self.core, 1, keepdims=False)
        other = self.swap(lax.dynamic_index_in_dim(tiles, 1 - self.core, 1, keepdims=False))
        halves = self.in_core_order(mine, other)
        outs, at = [], 0
        for _, cols in pack.narrow:
            t = cols // (2 * LANES)
            both = jnp.stack([h[at : at + t] for h in halves])
            outs.append(both.transpose(2, 0, 1, 3).reshape(rows, cols))
            at += t
        return outs

    def split_tall(self, total, pack):
        outs = []
        for (rows, cols), at in zip(pack.tall, pack.tall_at):
            own, t = rows // self.n, cols // LANES
            piece = total[at : at + t * own].reshape(t, own, LANES)
            outs.append(piece.transpose(1, 0, 2).reshape(own, cols))
        return outs


def on_device(
    device_count,
    tokens,
    cotangent,
    seq_lens,
    seq_starts,
    input_gain,
    w_query,
    w_key,
    w_value,
    query_gain,
    key_gain,
    w_output,
    attn_post_gain,
    ffn_pre_gain,
    w_gate,
    w_up,
    w_down,
    ffn_post_gain,
):
    mover = Mover(device_count)
    chips = mover.chips
    slots, model = tokens.shape
    hd = w_key.shape[1]
    heads = w_query.shape[1] // hd
    ffn = Pack(
        chips,
        [(model, w_gate.shape[1]), (model, w_up.shape[1])],
        [(w_output.shape[0] * device_count, model), (w_down.shape[0] * device_count, model)],
    )
    attn = Pack(chips, [(model, heads * hd), (model, hd), (model, hd)], [])

    gains = [input_gain, query_gain, key_gain, attn_post_gain, ffn_pre_gain, ffn_post_gain]
    flat = jnp.concatenate(gains)
    flat = jnp.pad(flat, (0, 8 * LANES - flat.shape[0])).reshape(8, LANES)
    narrow = mover.trade_halves([w_gate, w_up, w_query, w_key, w_value])
    split = w_gate.shape[1]
    far = lax.all_gather(mover.tiled([narrow[:, :split]]), AX, axis=0)
    gathered = far.reshape(chips, 2, ffn.wide_rows, LANES)
    down = list(reversed(range(mover.digits)))
    mine = mover.tiled([narrow[:, split:], flat])[None]
    tall = mover.tiled([w_output, w_down])[None]
    mine = jnp.concatenate(mover.spread(mine, down[0]), axis=0)
    for d in down[1:]:
        tall, mine = lax.optimization_barrier((tall, mine))
        tall = jnp.concatenate(mover.spread(tall, d + 1), axis=0)
        mine = jnp.concatenate(mover.spread(mine, d), axis=0)
    tall, mine = lax.optimization_barrier((tall, mine))
    tall = mover.spread(tall, 0)
    other = mover.swap(mine)
    both = jnp.stack(mover.in_core_order(mine[:, attn.used], other[:, attn.used]), axis=1)
    order = [int("".join(reversed(format_base4(k, mover.digits))), 4) for k in range(chips)]
    wanted = jnp.arange(chips, dtype=jnp.int32)[:, None] == (jnp.array(order, jnp.int32) ^ mover.chip)[None]
    flat = mm(wanted.astype(BF), both.reshape(chips, 2 * LANES)).reshape(device_count, LANES)
    vectors, at = [], 0
    for g in gains:
        vectors.append(flat[:, at : at + g.shape[0]].reshape(1, -1))
        at += g.shape[0]
    gin, gq, gk, gpost, gpre, gffn = vectors

    slot = jnp.arange(slots, dtype=jnp.int32)
    inside = (slot[None, :] >= seq_starts[:, None]) & (
        slot[None, :] < seq_starts[:, None] + seq_lens[:, None]
    )
    offset = jnp.sum(jnp.where(inside, seq_starts[:, None], 0), axis=0)
    frequency = rope_base ** (-2.0 * jnp.arange(hd // 2, dtype=F32) / hd)
    angles = (slot - offset).astype(F32)[:, None] * frequency[None, :]
    cos, sin = jnp.cos(angles), jnp.sin(angles)
    core = mover.core.astype(jnp.int32).reshape(1)

    place = jnp.stack([mover.core, mover.chip]).astype(jnp.int32)
    weights, h1, qraw, kraw, qn, kn, v, ob = run_forward(
        attn, heads, seq_lens, seq_starts, place, mine, other, tokens, cos, sin, gin, gq, gk
    )
    tall, ob = lax.optimization_barrier((tall, ob))
    tall_mine = jnp.concatenate(tall, axis=0)
    tall_other = mover.swap(tall_mine)
    result, dx1, dob, dgains, keep, send = run_middle(
        ffn, seq_lens, seq_starts, place, tall_mine, tall_other, gathered, tokens, ob, cotangent, gpost, gpre, gffn
    )
    up = list(range(mover.digits))
    cut = 3 * ffn.used // 32 * 8
    both = [mover.by_digits(keep), mover.by_digits(mover.swap(send))]
    near = mover.shares([v[..., :cut, :] for v in both], up[0], down)
    far = mover.total([v[..., cut:, :] for v in both]).astype(BF)
    dob, near, far = lax.optimization_barrier((dob, near, far))
    near = mover.trade(near, up[0])
    far = mover.scatter(far, down[0])
    grad_tokens, dgin, dgq, dgk, keep, send = run_backward(
        attn, heads, seq_lens, seq_starts, core, weights, tokens, dx1, h1, qraw, kraw, qn, dob, kn, v,
        cos, sin, gin, gq, gk,
    )
    dffn, dpre, dpost = (jnp.sum(dgains[i], axis=0) for i in range(3))
    grads = [jnp.sum(dgin, axis=0), jnp.sum(dgq, axis=0), jnp.sum(dgk, axis=0), dpost, dpre, dffn]
    flat = jnp.concatenate([g.reshape(device_count, -1) for g in grads], axis=1).astype(BF)
    flat = jnp.pad(flat, ((0, 0), (0, 8 * LANES - flat.shape[1]))).reshape(chips, 2, 8, LANES)
    keep = jnp.concatenate(
        [keep, lax.dynamic_index_in_dim(flat, mover.core, 1, keepdims=False)], axis=1
    )
    send = jnp.concatenate(
        [send, lax.dynamic_index_in_dim(flat, 1 - mover.core, 1, keepdims=False)], axis=1
    )
    send, near, far = lax.optimization_barrier((send, near, far))
    attn_parts = [mover.by_digits(keep), mover.by_digits(mover.swap(send))]
    for d in down[1:]:
        far = mover.scatter(far, d)
    for d in up:
        share = mover.shares(attn_parts, d, [k for k in down if k >= d])
        if d + 1 < mover.digits:
            near = mover.shares(near, d + 1, [k for k in down if k > d])
            share, near = lax.optimization_barrier((share, near))
            near = mover.trade(near, d + 1)
        attn_parts = mover.trade(share, d)
    far, attn_parts = lax.optimization_barrier((far, attn_parts))
    ffn_sum = jnp.concatenate([mover.total(near), far.astype(F32)], axis=0)
    attn_sum = mover.total(attn_parts)
    own_gate, own_up = mover.split_narrow(ffn_sum, ffn)
    own_output, own_down = mover.split_tall(ffn_sum, ffn)
    own_query, own_key, own_value = mover.split_narrow(attn_sum, attn)
    flat = attn_sum[attn.used :].reshape(-1)
    owned, at = [], 0
    for g in gains:
        owned.append(flat[at : at + g.shape[0]])
        at += g.shape[0]
    own_gin, own_gq, own_gk, own_gpost, own_gpre, own_gffn = owned
    return (
        result, grad_tokens, own_gin, own_query, own_key, own_value, own_gq, own_gk, own_output, own_gpost,
        own_gpre, own_gate, own_up, own_down, own_gffn,
    )


def solution(mesh):
    rows, flat = P(AX, None), P(AX)
    device_count = mesh.shape[AX]

    def block(*arrays):
        return on_device(device_count, *arrays)

    return jax.shard_map(
        block,
        mesh=mesh,
        in_specs=(
            rows, rows, flat, flat, flat, rows, rows, rows, flat, flat, rows, flat, flat, rows, rows, rows, flat,
        ),
        out_specs=(
            rows, rows, flat, rows, rows, rows, flat, flat, rows, flat, flat, rows, rows, rows, flat,
        ),
        check_vma=False,
    )
```
